512 devices in a mesh: row: 32 (over y, z_hi, core), col: 16 (over x, z_lo).
Axes of the slice: x: 4, y: 4, z: 16 (z_hi: 4, z_lo: 4; z = z_hi * 4 + z_lo), core: 2. Of those that a mesh axis runs over, the one named last changes fastest.
Arguments:
- site_cells: int32 [3, 1, 16384], P(None, None, 'row'), may hold values from 0 to 47
- site_scale: float32 [1, 16384], P(None, 'row'), may hold values from 0.3 to 3
- panel: int32 [1], replicated, may hold values from 0 to 31
Outputs:
- lower_panel: float32 [1, 16384, 512], P(None, 'row', 'col')
- trailing: bfloat16 [1, 16384, 2, 8192], P(None, 'row', None, 'col')
The draws below stay inside these ranges and needn't reach their ends.
All inputs are finite; a program needn't handle non-finite values.
Results may differ from the reference program's by a relative error of at most 0.002.
Values sent between devices are 32-bit elements; how exact they have to be, the bound alone decides.
A program may use at most 64 MiB of HBM per device.

```python
import math
import jax
import jax.numpy as jnp
from jax import lax

NB = 512
TR = 1
TC = 2
N_ROW = 32
N_COL = 16


def place_ends(drawn, stream_key, smallest, top_value):
    index_at = [jax.random.randint(jax.random.fold_in(stream_key, axis), (), 0, length) for axis, length in enumerate(drawn.shape)]
    widest = drawn.shape.index(max(drawn.shape))
    next_to = index_at[:widest] + [(index_at[widest] + 1) % drawn.shape[widest]] + index_at[widest + 1:]
    return drawn.at[tuple(index_at)].set(smallest).at[tuple(next_to)].set(top_value)


def steps_of(stream_key, shape, split, smallest, top_value):
    level = 1.0
    for axis_at, shards_of in split:
        draws = jax.random.uniform(jax.random.fold_in(jax.random.fold_in(stream_key, 6), axis_at), (shards_of,), jnp.float32, smallest / len(split), top_value / len(split))
        level = level * jnp.repeat(jnp.exp(draws), shape[axis_at] // shards_of).reshape((-1,) + (1,) * (len(shape) - 1 - axis_at))
    return level


def setup_inputs(seed: int = 0) -> dict:
    splits = jax.random.split(jax.random.key(seed), 4)
    return {
        "site_cells": place_ends(jax.random.randint(splits[0], (3, TR, N_ROW * NB), 0, 48), jax.random.fold_in(splits[0], 1), 0, 47).astype(jnp.int32),
        "site_scale": jnp.clip(jnp.exp(math.log(3.0) - 2.3025851 * jax.random.uniform(splits[1], (TR, N_ROW * NB), jnp.float32) ** steps_of(splits[1], (TR, N_ROW * NB), ((1, 32),), -0.2, 0.2)), 0.3, 3.0),
        "panel": jax.random.randint(splits[2], (1,), 0, TR * N_ROW).astype(jnp.int32),
    }


stretch = (1.0, 1.0, 2.0)
nugget = 0.25
inv_length = 1.7320508075688772 / 12.0

def covariance(row_cells, row_scale, row_index, col_cells, col_scale, col_index):
    squared = jnp.zeros((row_cells.shape[1], col_cells.shape[1]), jnp.float32)
    for axis_id in range(3):
        delta = (row_cells[axis_id][:, None] - col_cells[axis_id][None, :]) * stretch[axis_id]
        squared = squared + delta * delta
    radius = inv_length * jnp.sqrt(squared)
    kernel = (1.0 + radius) * jnp.exp(-radius)
    kernel = kernel + nugget * (row_index[:, None] == col_index[None, :]).astype(jnp.float32)
    return row_scale[:, None] * col_scale[None, :] * kernel

def reference(site_cells, site_scale, panel):
    tiles = TR * N_ROW
    cells = site_cells.astype(jnp.float32).reshape(3, tiles * NB)
    scales = site_scale.reshape(tiles * NB)
    index = jnp.arange(tiles * NB, dtype=jnp.int32)
    pivot = panel[0]
    start = (pivot * NB).astype(jnp.int32)
    piv_cells = lax.dynamic_slice_in_dim(cells, start, NB, 1)
    piv_scale = lax.dynamic_slice_in_dim(scales, start, NB, 0)
    piv_index = lax.dynamic_slice_in_dim(index, start, NB, 0)
    block = covariance(piv_cells, piv_scale, piv_index, piv_cells, piv_scale, piv_index)
    factor = jnp.linalg.cholesky(block)
    inverse = jax.scipy.linalg.solve_triangular(factor, jnp.eye(NB, dtype=jnp.float32), lower=True)

    def panel_tile(tile):
        first = (tile * NB).astype(jnp.int32)
        rows = covariance(lax.dynamic_slice_in_dim(cells, first, NB, 1), lax.dynamic_slice_in_dim(scales, first, NB, 0), lax.dynamic_slice_in_dim(index, first, NB, 0), piv_cells, piv_scale, piv_index)
        return jnp.dot(rows, inverse.T, precision=lax.Precision.HIGHEST)
    lower = lax.map(panel_tile, jnp.arange(tiles, dtype=jnp.int32))
    lower_flat = lower.reshape(tiles * NB, NB)

    def trailing_tile(tile):
        first = (tile * NB).astype(jnp.int32)
        rows = covariance(lax.dynamic_slice_in_dim(cells, first, NB, 1), lax.dynamic_slice_in_dim(scales, first, NB, 0), lax.dynamic_slice_in_dim(index, first, NB, 0), cells, scales, index)
        mine = lax.dynamic_index_in_dim(lower, tile, 0, keepdims=False)
        return (rows - jnp.dot(mine, lower_flat.T, precision=lax.Precision.HIGHEST)).astype(jnp.bfloat16)
    update = lax.map(trailing_tile, jnp.arange(tiles, dtype=jnp.int32))
    return (lower.reshape(TR, N_ROW * NB, NB), update.reshape(TR, N_ROW * NB, TC, N_COL * NB))
```

```python
import math
import jax
import jax.numpy as jnp
from jax import lax
from jax.experimental import pallas as pl
from jax.experimental.pallas import tpu as pltpu
from jax.sharding import PartitionSpec as P

NUGGET = 0.25
DECAY = 1.7320508075688772 / 12.0 / math.log(2.0)
LN2 = math.log(2.0)
HI = lax.Precision.HIGHEST
PART = 128
ROWS = 8


def dot(a, b, precision=HI):
    return jnp.dot(a, b, precision=precision, preferred_element_type=jnp.float32)


def dot_tn(a, b, precision=HI):
    return lax.dot_general(a, b, (((0,), (0,)), ((), ())), precision=precision, preferred_element_type=jnp.float32)


def features(tile):
    x, y, z = tile[0:1], tile[1:2], 2.0 * tile[2:3]
    norm = x * x + y * y + z * z
    high = jnp.floor(norm * (1.0 / 256.0)) * 256.0
    low = norm - high
    one, zero = jnp.ones_like(x), jnp.zeros_like(x)
    left = jnp.concatenate([x, y, z, high, low, one, one, zero], axis=0)
    right = jnp.concatenate([-2.0 * x, -2.0 * y, -2.0 * z, one, one, high, low, zero], axis=0)
    return left, right


def matern(left, right):
    squared = dot_tn(left, right, lax.Precision.DEFAULT)
    t = squared * lax.rsqrt(jnp.maximum(squared, 0.5)) * DECAY
    return (1.0 + t * LN2) * jnp.exp2(-t)


def eye(n, value):
    a = lax.broadcasted_iota(jnp.int32, (n, n), 0)
    b = lax.broadcasted_iota(jnp.int32, (n, n), 1)
    return jnp.where(a == b, value, 0.0)


def inverse_factor(block):
    groups = PART // ROWS
    shape = (ROWS, PART)
    sub = lax.broadcasted_iota(jnp.int32, shape, 0)
    lane = lax.broadcasted_iota(jnp.int32, shape, 1)
    a = [block(g) for g in range(groups)]
    e = [jnp.where(lane == sub + g * ROWS, 1.0, 0.0) for g in range(groups)]

    def col(x, k):
        return jnp.broadcast_to(x[:, k : k + 1], shape)

    def row(x, j):
        return jnp.broadcast_to(x[j : j + 1, :], shape)

    out = []
    for p in range(groups):
        c = [col(a[p], p * ROWS + k) for k in range(ROWS)]
        inv, rows_c, rows_a, rows_e = [], [], [], []
        diag = jnp.ones(shape, jnp.float32)
        for j in range(ROWS):
            d = row(c[j], j)
            diag = jnp.where(sub == j, d, diag)
            inv.append(1.0 / d)
            rows_c.append([row(c[k], j) for k in range(j + 1, ROWS)])
            rows_a.append(row(a[p], j))
            rows_e.append(row(e[p], j))
            if j < ROWS - 1:
                m = jnp.where(sub > j, c[j] * inv[j], 0.0)
                for k in range(j + 1, ROWS):
                    c[k] = c[k] - m * rows_c[j][k - j - 1]
                a[p] = a[p] - m * rows_a[j]
                e[p] = e[p] - m * rows_e[j]
        out.append(e[p] * lax.rsqrt(diag))
        for g in range(p + 1, groups):
            c = [col(a[g], p * ROWS + k) for k in range(ROWS)]
            for j in range(ROWS):
                m = c[j] * inv[j]
                for k in range(j + 1, ROWS):
                    c[k] = c[k] - m * rows_c[j][k - j - 1]
                a[g] = a[g] - m * rows_a[j]
                e[g] = e[g] - m * rows_e[j]
    return out


def eliminate(t_ref, d_ref):
    n = t_ref.shape[0]
    steps = n // PART

    def step(i, carry):
        base = pl.multiple_of(i * PART, PART)
        for k in range(steps):
            @pl.when(i == k)
            def _():
                d_ref[...] = t_ref[k * PART:(k + 1) * PART, k * PART:(k + 1) * PART]
        out = inverse_factor(lambda g: d_ref[g * ROWS:(g + 1) * ROWS, :])
        for g, v in enumerate(out):
            d_ref[g * ROWS:(g + 1) * ROWS, :] = v
        for k in range(steps):
            @pl.when(i == k)
            def _():
                lo, hi = k * PART, (k + 1) * PART
                small = d_ref[...]
                if k > 0:
                    t_ref[lo:hi, :lo] = dot(small, t_ref[lo:hi, :lo])
                t_ref[lo:hi, lo:hi] = small
                if hi < n:
                    right = dot(small, t_ref[lo:hi, hi:])
                    t_ref[hi:, :hi] = jnp.concatenate([t_ref[hi:, :lo], jnp.zeros((n - hi, PART), jnp.float32)], axis=1) - dot_tn(right, t_ref[lo:hi, :hi]) if lo else -dot_tn(right, small)
                    t_ref[hi:, hi:] = t_ref[hi:, hi:] - dot_tn(right, right)
                    t_ref[lo:hi, hi:] = jnp.zeros((PART, n - hi), jnp.float32)
        return carry

    lax.fori_loop(0, steps, step, 0)


def body(p_ref, all_ref, panel_ref, trail_ref, t_ref, d_ref, k_ref):
    width = panel_ref.shape[0]
    share = panel_ref.shape[1]
    my_row = lax.axis_index("row")
    my_col = lax.axis_index("col")
    n_col = lax.axis_size("col")
    pivot = p_ref[0]

    def tile(t):
        return all_ref[:, pl.ds(pl.multiple_of(t * width, width), width)]

    piv = tile(pivot)
    mine = tile(my_row)
    cols = [tile(my_col + m * n_col) for m in range(trail_ref.shape[1])]
    col_ids = [my_col + m * n_col for m in range(trail_ref.shape[1])]
    piv_left, piv_right = features(piv)
    t_ref[...] = matern(piv_left, piv_right) + eye(width, NUGGET)
    eliminate(t_ref, d_ref)
    my_left, my_right = features(mine)

    def nugget(same):
        return eye(width, jnp.where(same, NUGGET, 0.0))

    k_ref[:, :width] = matern(piv_left, my_right) + nugget(my_row == pivot)
    for m, (one, tid) in enumerate(zip(cols, col_ids)):
        k_ref[:, (m + 1) * width:(m + 2) * width] = matern(piv_left, features(one)[1]) + nugget(tid == pivot)
    mine_t = mine.T
    scale_r = mine_t[:, 3:4]
    some = t_ref[pl.ds(pl.multiple_of(my_col * share, share), share), :]
    panel_ref[...] = dot(some, k_ref[:, :width]).T * scale_r
    half = width // 2
    low = dot(t_ref[half:, :], k_ref[...])
    k_ref[:half] = dot(t_ref[:half, :half], k_ref[:half])
    k_ref[half:] = low
    x_r = k_ref[:, :width].T
    for m, (one, tid) in enumerate(zip(cols, col_ids)):
        prior = matern(my_left, features(one)[1]) + nugget(tid == my_row)
        rest = prior - dot(x_r, k_ref[:, (m + 1) * width:(m + 2) * width])
        trail_ref[:, m, :] = (rest * (scale_r * one[3:4])).astype(jnp.bfloat16)


def on_device(site_cells, site_scale, panel):
    width = site_cells.shape[2]
    n_row = lax.axis_size("row")
    n_col = lax.axis_size("col")
    tiles = n_row * site_cells.shape[1]
    sites = jnp.concatenate([site_cells[:, 0, :].astype(jnp.float32), site_scale], axis=0)
    sites = lax.all_gather(sites, "row", axis=1, tiled=True)
    parts = tiles // n_col
    panel_out, trailing = pl.pallas_call(
        body,
        out_shape=(
            jax.ShapeDtypeStruct((width, width // n_col), jnp.float32),
            jax.ShapeDtypeStruct((width, parts, width), jnp.bfloat16),
        ),
        in_specs=[pl.BlockSpec(memory_space=pltpu.SMEM), pl.BlockSpec(memory_space=pltpu.VMEM)],
        out_specs=[pl.BlockSpec(memory_space=pltpu.VMEM)] * 2,
        scratch_shapes=[
            pltpu.VMEM((width, width), jnp.float32),
            pltpu.VMEM((PART, PART), jnp.float32),
            pltpu.VMEM((width, (parts + 1) * width), jnp.float32),
        ],
        compiler_params=pltpu.CompilerParams(vmem_limit_bytes=48 << 20),
        name="eliminate_panel",
    )(panel, sites)
    return panel_out[None], trailing[None]


def solution(mesh):
    placed = (P(None, None, "row"), P(None, "row"), P())
    return jax.shard_map(
        on_device,
        mesh=mesh,
        in_specs=placed,
        out_specs=(P(None, "row", "col"), P(None, "row", None, "col")),
        check_vma=False,
    )
```

```python
import math
import jax
import jax.numpy as jnp
from jax import lax
from jax.experimental import pallas as pl
from jax.experimental.pallas import tpu as pltpu
from jax.sharding import PartitionSpec as P

MESH = pl.DeviceIdType.MESH
NUGGET = 0.25
DECAY = 1.7320508075688772 / 12.0 / math.log(2.0)
LN2 = math.log(2.0)
HI = lax.Precision.HIGHEST
PART = 128
ROWS = 8


def dot(a, b, precision=HI):
    return jnp.dot(a, b, precision=precision, preferred_element_type=jnp.float32)


def dot_tn(a, b, precision=HI):
    return lax.dot_general(a, b, (((0,), (0,)), ((), ())), precision=precision, preferred_element_type=jnp.float32)


def features(tile):
    x, y, z = tile[0:1], tile[1:2], 2.0 * tile[2:3]
    norm = x * x + y * y + z * z
    high = jnp.floor(norm * (1.0 / 256.0)) * 256.0
    low = norm - high
    one, zero = jnp.ones_like(x), jnp.zeros_like(x)
    left = jnp.concatenate([x, y, z, high, low, one, one, zero], axis=0)
    right = jnp.concatenate([-2.0 * x, -2.0 * y, -2.0 * z, one, one, high, low, zero], axis=0)
    return left, right


def matern(left, right):
    squared = dot_tn(left, right, lax.Precision.DEFAULT)
    t = squared * lax.rsqrt(jnp.maximum(squared, 0.5)) * DECAY
    return (1.0 + t * LN2) * jnp.exp2(-t)


def eye(n, value):
    a = lax.broadcasted_iota(jnp.int32, (n, n), 0)
    b = lax.broadcasted_iota(jnp.int32, (n, n), 1)
    return jnp.where(a == b, value, 0.0)


def inverse_factor(block):
    groups = PART // ROWS
    shape = (ROWS, PART)
    sub = lax.broadcasted_iota(jnp.int32, shape, 0)
    lane = lax.broadcasted_iota(jnp.int32, shape, 1)
    a = [block(g) for g in range(groups)]
    e = [jnp.where(lane == sub + g * ROWS, 1.0, 0.0) for g in range(groups)]

    def col(x, k):
        return jnp.broadcast_to(x[:, k : k + 1], shape)

    def row(x, j):
        return jnp.broadcast_to(x[j : j + 1, :], shape)

    out = []
    for p in range(groups):
        c = [col(a[p], p * ROWS + k) for k in range(ROWS)]
        inv, rows_c, rows_a, rows_e = [], [], [], []
        diag = jnp.ones(shape, jnp.float32)
        for j in range(ROWS):
            d = row(c[j], j)
            diag = jnp.where(sub == j, d, diag)
            inv.append(1.0 / d)
            rows_c.append([row(c[k], j) for k in range(j + 1, ROWS)])
            rows_a.append(row(a[p], j))
            rows_e.append(row(e[p], j))
            if j < ROWS - 1:
                m = jnp.where(sub > j, c[j] * inv[j], 0.0)
                for k in range(j + 1, ROWS):
                    c[k] = c[k] - m * rows_c[j][k - j - 1]
                a[p] = a[p] - m * rows_a[j]
                e[p] = e[p] - m * rows_e[j]
        out.append(e[p] * lax.rsqrt(diag))
        for g in range(p + 1, groups):
            c = [col(a[g], p * ROWS + k) for k in range(ROWS)]
            for j in range(ROWS):
                m = c[j] * inv[j]
                for k in range(j + 1, ROWS):
                    c[k] = c[k] - m * rows_c[j][k - j - 1]
                a[g] = a[g] - m * rows_a[j]
                e[g] = e[g] - m * rows_e[j]
    return out


def eliminate(t_ref, d_ref):
    n = t_ref.shape[0]
    steps = n // PART

    def step(i, carry):
        base = pl.multiple_of(i * PART, PART)
        for k in range(steps):
            @pl.when(i == k)
            def _():
                d_ref[...] = t_ref[k * PART:(k + 1) * PART, k * PART:(k + 1) * PART]
        out = inverse_factor(lambda g: d_ref[g * ROWS:(g + 1) * ROWS, :])
        for g, v in enumerate(out):
            d_ref[g * ROWS:(g + 1) * ROWS, :] = v
        for k in range(steps):
            @pl.when(i == k)
            def _():
                lo, hi = k * PART, (k + 1) * PART
                small = d_ref[...]
                if k > 0:
                    t_ref[lo:hi, :lo] = dot(small, t_ref[lo:hi, :lo])
                t_ref[lo:hi, lo:hi] = small
                if hi < n:
                    right = dot(small, t_ref[lo:hi, hi:])
                    t_ref[hi:, :hi] = jnp.concatenate([t_ref[hi:, :lo], jnp.zeros((n - hi, PART), jnp.float32)], axis=1) - dot_tn(right, t_ref[lo:hi, :hi]) if lo else -dot_tn(right, small)
                    t_ref[hi:, hi:] = t_ref[hi:, hi:] - dot_tn(right, right)
                    t_ref[lo:hi, hi:] = jnp.zeros((PART, n - hi), jnp.float32)
        return carry

    lax.fori_loop(0, steps, step, 0)


def gather_body(p_ref, cells_ref, scale_ref, out_ref, line_ref, plane_ref, line_send, line_recv, plane_send, plane_recv):
    my_row = lax.axis_index("row")
    my_col = lax.axis_index("col")
    n_line, n_plane = line_ref.shape[0], plane_ref.shape[0]
    core = lax.rem(my_row, 2)
    deep = lax.rem(lax.div(my_row, 2), n_line)
    flat = lax.div(my_row, 2 * n_line) * 2 + core

    def row_of(flat_at, deep_at):
        return lax.div(flat_at, 2) * (2 * n_line) + deep_at * 2 + lax.rem(flat_at, 2)

    def ahead(k):
        return row_of(flat, lax.rem(deep + k, n_line))

    def aside(k):
        return row_of(lax.rem(flat + k, n_plane), deep)

    barrier = pltpu.get_barrier_semaphore()
    for k in range(1, n_line):
        pl.semaphore_signal(barrier, inc=1, device_id={"row": ahead(k)}, device_id_type=MESH)
    for k in range(1, n_plane):
        pl.semaphore_signal(barrier, inc=1, device_id={"row": aside(k)}, device_id_type=MESH)
    for axis in range(3):
        line_ref[0, axis:axis + 1] = cells_ref[axis].astype(jnp.float32)
    line_ref[0, 3:4] = scale_ref[...]
    pl.semaphore_wait(barrier, n_line + n_plane - 2)

    line = []
    for k in range(1, n_line):
        copy = pltpu.make_async_remote_copy(
            src_ref=line_ref.at[0], dst_ref=line_ref.at[k],
            send_sem=line_send.at[k], recv_sem=line_recv.at[k],
            device_id={"row": ahead(k)}, device_id_type=MESH,
        )
        copy.start()
        line.append(copy)
    for copy in line:
        copy.wait()
    pivot = p_ref[0]
    n_col = lax.axis_size("col")
    col_deep = lax.rem(lax.div(my_col, 2), n_line)
    chosen = jnp.zeros(line_ref.shape[1:], jnp.float32)
    column = jnp.zeros(line_ref.shape[1:], jnp.float32)
    for k in range(n_line):
        deep_at = lax.rem(deep + n_line - k, n_line)
        held = line_ref[k]
        chosen = jnp.where(row_of(flat, deep_at) == pivot, held, chosen)
        column = jnp.where(deep_at == col_deep, held, column)
    plane_ref[0, 0] = chosen
    plane_ref[0, 1] = column
    plane = []
    for k in range(1, n_plane):
        copy = pltpu.make_async_remote_copy(
            src_ref=plane_ref.at[0], dst_ref=plane_ref.at[k],
            send_sem=plane_send.at[k], recv_sem=plane_recv.at[k],
            device_id={"row": aside(k)}, device_id_type=MESH,
        )
        copy.start()
        plane.append(copy)
    for copy in plane:
        copy.wait()
    parts = out_ref.shape[0] - 2
    results = [jnp.zeros(line_ref.shape[1:], jnp.float32) for _ in range(parts + 1)]
    for k in range(n_plane):
        flat_at = lax.rem(flat + n_plane - k, n_plane)
        results[0] = results[0] + plane_ref[k, 0]
        for m in range(parts):
            tile = my_col + m * n_col
            home = lax.div(tile, 2 * n_line) * 2 + lax.rem(tile, 2)
            results[m + 1] = jnp.where(flat_at == home, plane_ref[k, 1], results[m + 1])
    out_ref[0] = results[0]
    out_ref[1] = line_ref[0]
    for m in range(parts):
        out_ref[m + 2] = results[m + 1]


def gather_sites(cells, scale, panel):
    width = cells.shape[2]
    n_line = 4
    n_plane = lax.axis_size("row") // n_line
    parts = lax.axis_size("row") // lax.axis_size("col")
    return pl.pallas_call(
        gather_body,
        out_shape=jax.ShapeDtypeStruct((parts + 2, 4, width), jnp.float32),
        in_specs=[pl.BlockSpec(memory_space=pltpu.SMEM)] + [pl.BlockSpec(memory_space=pltpu.VMEM)] * 2,
        out_specs=pl.BlockSpec(memory_space=pltpu.VMEM),
        scratch_shapes=[
            pltpu.VMEM((n_line, 4, width), jnp.float32),
            pltpu.VMEM((n_plane, 2, 4, width), jnp.float32),
            pltpu.SemaphoreType.DMA((n_line,)),
            pltpu.SemaphoreType.DMA((n_line,)),
            pltpu.SemaphoreType.DMA((n_plane,)),
            pltpu.SemaphoreType.DMA((n_plane,)),
        ],
        compiler_params=pltpu.CompilerParams(collective_id=0, has_side_effects=True),
        name="gather_sites",
    )(panel, cells, scale)


def body(p_ref, all_ref, panel_ref, trail_ref, t_ref, d_ref, k_ref):
    share, width = panel_ref.shape
    my_row = lax.axis_index("row")
    my_col = lax.axis_index("col")
    n_col = lax.axis_size("col")
    pivot = p_ref[0]

    piv, mine = all_ref[0], all_ref[1]
    cols = [all_ref[m + 2] for m in range(trail_ref.shape[1])]
    col_ids = [my_col + m * n_col for m in range(trail_ref.shape[1])]
    piv_left, piv_right = features(piv)
    t_ref[...] = matern(piv_left, piv_right) + eye(width, NUGGET)
    eliminate(t_ref, d_ref)
    my_left, my_right = features(mine)

    def nugget(same):
        return eye(width, jnp.where(same, NUGGET, 0.0))

    k_ref[:, :width] = matern(piv_left, my_right) + nugget(my_row == pivot)
    for m, (one, tid) in enumerate(zip(cols, col_ids)):
        k_ref[:, (m + 1) * width:(m + 2) * width] = matern(piv_left, features(one)[1]) + nugget(tid == pivot)
    mine_t = mine.T
    scale_r = mine_t[:, 3:4]
    some = t_ref[pl.ds(pl.multiple_of(my_col * share, share), share), :]
    panel_ref[...] = dot(some, k_ref[:, :width]) * mine[3:4]
    half = width // 2
    low = dot(t_ref[half:, :], k_ref[...])
    k_ref[:half] = dot(t_ref[:half, :half], k_ref[:half])
    k_ref[half:] = low
    x_r = k_ref[:, :width].T
    for m, (one, tid) in enumerate(zip(cols, col_ids)):
        prior = matern(my_left, features(one)[1]) + nugget(tid == my_row)
        rest = prior - dot(x_r, k_ref[:, (m + 1) * width:(m + 2) * width])
        trail_ref[:, m, :] = (rest * (scale_r * one[3:4])).astype(jnp.bfloat16)


def on_device(site_cells, site_scale, panel):
    width = site_cells.shape[2]
    n_row = lax.axis_size("row")
    n_col = lax.axis_size("col")
    sites = gather_sites(site_cells, site_scale, panel)
    parts = n_row // n_col
    panel_out, trailing = pl.pallas_call(
        body,
        out_shape=(
            jax.ShapeDtypeStruct((width // n_col, width), jnp.float32),
            jax.ShapeDtypeStruct((width, parts, width), jnp.bfloat16),
        ),
        in_specs=[pl.BlockSpec(memory_space=pltpu.SMEM), pl.BlockSpec(memory_space=pltpu.VMEM)],
        out_specs=[pl.BlockSpec(memory_space=pltpu.VMEM)] * 2,
        scratch_shapes=[
            pltpu.VMEM((width, width), jnp.float32),
            pltpu.VMEM((PART, PART), jnp.float32),
            pltpu.VMEM((width, (parts + 1) * width), jnp.float32),
        ],
        compiler_params=pltpu.CompilerParams(vmem_limit_bytes=48 << 20),
        name="eliminate_panel",
    )(panel, sites)
    return panel_out.T[None], trailing[None]


def solution(mesh):
    placed = (P(None, None, "row"), P(None, "row"), P())
    return jax.shard_map(
        on_device,
        mesh=mesh,
        in_specs=placed,
        out_specs=(P(None, "row", "col"), P(None, "row", None, "col")),
        check_vma=False,
    )
```

```python
import math
import jax
import jax.numpy as jnp
from jax import lax
from jax.experimental import pallas as pl
from jax.experimental.pallas import tpu as pltpu
from jax.sharding import PartitionSpec as P

MESH = pl.DeviceIdType.MESH
NUGGET = 0.25
INV_LENGTH = 1.7320508075688772 / 12.0
LOG2E = 1.0 / math.log(2.0)
HI = lax.Precision.HIGHEST
PART = 128
HALF = 64
ROWS = 8


def dot(a, b, precision=HI):
    return jnp.dot(a, b, precision=precision, preferred_element_type=jnp.float32)


def dot_tn(a, b, precision=HI):
    return lax.dot_general(a, b, (((0,), (0,)), ((), ())), precision=precision, preferred_element_type=jnp.float32)


def split(a):
    high = a.astype(jnp.bfloat16)
    return high, (a - high.astype(jnp.float32)).astype(jnp.bfloat16)


def features(tile):
    x, y, z = tile[0:1], tile[1:2], 2.0 * tile[2:3]
    norm = x * x + y * y + z * z
    high = jnp.floor(norm * (1.0 / 256.0)) * 256.0
    low = norm - high
    one, zero = jnp.ones_like(x), jnp.zeros_like(x)
    left = jnp.concatenate([x, y, z, high, low, one, one, zero], axis=0)
    right = jnp.concatenate([-2.0 * x, -2.0 * y, -2.0 * z, one, one, high, low, zero], axis=0)
    return left, right


def squared(left, right):
    return dot_tn(left, right, lax.Precision.DEFAULT)


def matern(squares):
    radius = squares * lax.rsqrt(jnp.maximum(squares, 0.5)) * INV_LENGTH
    return (1.0 + radius) * jnp.exp2(radius * -LOG2E)


def col(x, k):
    return jnp.broadcast_to(x[:, k:k + 1], (ROWS, PART))


def row(x, j):
    return jnp.broadcast_to(x[j:j + 1, :], (ROWS, PART))


def inverse_factor(block, beside):
    groups, half = PART // ROWS, HALF // ROWS
    sub = lax.broadcasted_iota(jnp.int32, (ROWS, PART), 0)
    lane = lax.broadcasted_iota(jnp.int32, (ROWS, PART), 1)
    t = [block(g) for g in range(groups)]
    out = []
    for base in range(0, groups, half):
        top = base + half
        raw = []
        c = [col(t[base], base * ROWS + k) for k in range(ROWS)]
        for p in range(base, top):
            lo = p * ROWS
            inside = jnp.logical_and(lane >= lo, lane < lo + ROWS)
            steps = []
            diag = jnp.ones((ROWS, PART), jnp.float32)
            own = jnp.where(inside, jnp.where(lane - lo == sub, 1.0, 0.0), t[p])
            last = p + 1 == top
            if not last:
                cc = [col(t[p + 1], lo + k) for k in range(ROWS)]
                cn = [col(t[p + 1], lo + ROWS + k) for k in range(ROWS)]
                tg = jnp.where(inside, 0.0, t[p + 1])
            for j in range(ROWS):
                d = row(c[j], j)
                diag = jnp.where(sub == j, d, diag)
                inv = 1.0 / d
                rc = [row(c[k], j) for k in range(j + 1, ROWS)]
                ra = row(own, j)
                steps.append((inv, rc, ra))
                if j < ROWS - 1:
                    m = jnp.where(sub > j, c[j] * inv, 0.0)
                    for k in range(j + 1, ROWS):
                        c[k] = c[k] - m * rc[k - j - 1]
                    own = own - m * ra
                if not last:
                    m = cc[j] * inv
                    for k in range(ROWS):
                        cn[k] = cn[k] - m * row(cc[j], k)
                    for k in range(j + 1, ROWS):
                        cc[k] = cc[k] - m * rc[k - j - 1]
                    tg = tg - m * ra
            raw.append(own * lax.rsqrt(diag))
            beside()
            if last:
                break
            t[p + 1] = tg
            c = cn
            for g in range(p + 2, top):
                cc = [col(t[g], lo + k) for k in range(ROWS)]
                tg = jnp.where(inside, 0.0, t[g])
                for j in range(ROWS):
                    inv, rc, ra = steps[j]
                    m = cc[j] * inv
                    for k in range(j + 1, ROWS):
                        cc[k] = cc[k] - m * rc[k - j - 1]
                    tg = tg - m * ra
                t[g] = tg
        for i, r in enumerate(raw):
            out.append(jnp.where(lane < (base + i + 1) * ROWS, r, 0.0))
        if top < groups:
            done = top * ROWS
            u = jnp.concatenate(
                [jnp.where(jnp.logical_or(lane < (base + i + 1) * ROWS, lane >= done), r, 0.0) for i, r in enumerate(raw)],
                axis=0,
            )
            update = dot_tn(u[:, done:], u)
            for g in range(top, groups):
                keep = jnp.where(jnp.logical_and(lane >= base * ROWS, lane < done), 0.0, t[g])
                t[g] = keep - update[(g - top) * ROWS:(g - top + 1) * ROWS]
    return jnp.concatenate(out, axis=0)


def eliminate(t_ref, beside, done):
    n = t_ref.shape[0]
    for lo in range(0, n, PART):
        hi = lo + PART
        small = inverse_factor(lambda g: t_ref[lo + g * ROWS:lo + (g + 1) * ROWS, lo:hi], beside)
        left = jnp.concatenate([dot(small, t_ref[lo:hi, :lo]), small], axis=1) if lo else small
        if hi < n:
            after = hi + PART
            right = dot(small, t_ref[lo:hi, hi:after])
            t_ref[hi:after, hi:after] = t_ref[hi:after, hi:after] - dot_tn(right, right)
            if after < n:
                far = dot(small, t_ref[lo:hi, after:])
                t_ref[hi:after, after:] = t_ref[hi:after, after:] - dot_tn(right, far)
                t_ref[after:, after:] = t_ref[after:, after:] - dot_tn(far, far)
                right = jnp.concatenate([right, far], axis=1)
            update = dot_tn(right, left)
            if lo:
                t_ref[hi:, :lo] = t_ref[hi:, :lo] - update[:, :lo]
            t_ref[hi:, lo:hi] = -update[:, lo:]
            t_ref[lo:hi, hi:] = jnp.zeros((PART, n - hi), jnp.float32)
        t_ref[lo:hi, :hi] = left
        done(lo, hi, left)


def gather_body(p_ref, cells_ref, scale_ref, out_ref, line_ref, plane_ref, line_send, line_recv, plane_send, plane_recv):
    my_row = lax.axis_index("row")
    my_col = lax.axis_index("col")
    n_line, n_plane = line_ref.shape[0], plane_ref.shape[0]
    core = lax.rem(my_row, 2)
    deep = lax.rem(lax.div(my_row, 2), n_line)
    flat = lax.div(my_row, 2 * n_line) * 2 + core

    def row_of(flat_at, deep_at):
        return lax.div(flat_at, 2) * (2 * n_line) + deep_at * 2 + lax.rem(flat_at, 2)

    def ahead(k):
        return row_of(flat, lax.rem(deep + k, n_line))

    def aside(k):
        return row_of(lax.rem(flat + k, n_plane), deep)

    barrier = pltpu.get_barrier_semaphore()
    for k in range(1, n_line):
        pl.semaphore_signal(barrier, inc=1, device_id={"row": ahead(k)}, device_id_type=MESH)
    for k in range(1, n_plane):
        pl.semaphore_signal(barrier, inc=1, device_id={"row": aside(k)}, device_id_type=MESH)
    for axis in range(3):
        line_ref[0, axis:axis + 1] = cells_ref[axis].astype(jnp.float32)
    line_ref[0, 3:4] = scale_ref[...]
    pl.semaphore_wait(barrier, n_line + n_plane - 2)

    line = []
    for k in range(1, n_line):
        copy = pltpu.make_async_remote_copy(
            src_ref=line_ref.at[0], dst_ref=line_ref.at[k],
            send_sem=line_send.at[k], recv_sem=line_recv.at[k],
            device_id={"row": ahead(k)}, device_id_type=MESH,
        )
        copy.start()
        line.append(copy)
    for copy in line:
        copy.wait()
    pivot = p_ref[0]
    n_col = lax.axis_size("col")
    col_deep = lax.rem(lax.div(my_col, 2), n_line)
    chosen = jnp.zeros(line_ref.shape[1:], jnp.float32)
    column = jnp.zeros(line_ref.shape[1:], jnp.float32)
    for k in range(n_line):
        deep_at = lax.rem(deep + n_line - k, n_line)
        held = line_ref[k]
        chosen = jnp.where(row_of(flat, deep_at) == pivot, held, chosen)
        column = jnp.where(deep_at == col_deep, held, column)
    plane_ref[0, 0] = chosen
    plane_ref[0, 1] = column
    plane = []
    for k in range(1, n_plane):
        copy = pltpu.make_async_remote_copy(
            src_ref=plane_ref.at[0], dst_ref=plane_ref.at[k],
            send_sem=plane_send.at[k], recv_sem=plane_recv.at[k],
            device_id={"row": aside(k)}, device_id_type=MESH,
        )
        copy.start()
        plane.append(copy)
    for copy in plane:
        copy.wait()
    parts = out_ref.shape[0] - 2
    results = [jnp.zeros(line_ref.shape[1:], jnp.float32) for _ in range(parts + 1)]
    for k in range(n_plane):
        flat_at = lax.rem(flat + n_plane - k, n_plane)
        results[0] = results[0] + plane_ref[k, 0]
        for m in range(parts):
            tile = my_col + m * n_col
            home = lax.div(tile, 2 * n_line) * 2 + lax.rem(tile, 2)
            results[m + 1] = jnp.where(flat_at == home, plane_ref[k, 1], results[m + 1])
    out_ref[0] = results[0]
    out_ref[1] = line_ref[0]
    for m in range(parts):
        out_ref[m + 2] = results[m + 1]


def gather_sites(cells, scale, panel):
    width = cells.shape[2]
    n_line = 4
    n_plane = lax.axis_size("row") // n_line
    parts = lax.axis_size("row") // lax.axis_size("col")
    return pl.pallas_call(
        gather_body,
        out_shape=jax.ShapeDtypeStruct((parts + 2, 4, width), jnp.float32),
        in_specs=[pl.BlockSpec(memory_space=pltpu.SMEM)] + [pl.BlockSpec(memory_space=pltpu.VMEM)] * 2,
        out_specs=pl.BlockSpec(memory_space=pltpu.VMEM),
        scratch_shapes=[
            pltpu.VMEM((n_line, 4, width), jnp.float32),
            pltpu.VMEM((n_plane, 2, 4, width), jnp.float32),
            pltpu.SemaphoreType.DMA((n_line,)),
            pltpu.SemaphoreType.DMA((n_line,)),
            pltpu.SemaphoreType.DMA((n_plane,)),
            pltpu.SemaphoreType.DMA((n_plane,)),
        ],
        compiler_params=pltpu.CompilerParams(collective_id=0, has_side_effects=True),
        name="gather_sites",
    )(panel, cells, scale)


def body(p_ref, sites_ref, panel_ref, trail_ref, t_ref, k_ref, f_ref, x_ref):
    share, width = panel_ref.shape
    parts = trail_ref.shape[1]
    my_row = lax.axis_index("row")
    my_col = lax.axis_index("col")
    n_col = lax.axis_size("col")
    pivot = p_ref[0]
    piv, mine = sites_ref[0], sites_ref[1]
    cols = [sites_ref[m + 2] for m in range(parts)]
    col_ids = [my_col + m * n_col for m in range(parts)]
    piv_left, piv_right = features(piv)
    my_left, my_right = features(mine)
    rights = [my_right] + [features(one)[1] for one in cols]
    sub = lax.broadcasted_iota(jnp.int32, (width, width), 0)
    lane = lax.broadcasted_iota(jnp.int32, (width, width), 1)
    t_ref[...] = matern(squared(piv_left, piv_right)) + jnp.where(sub == lane, NUGGET, 0.0)
    for m, right in enumerate(rights):
        k_ref[:, m * width:(m + 1) * width] = squared(piv_left, right)
        if m:
            f_ref[:, (m - 1) * width:m * width] = squared(my_left, right)
    scale_r = mine.T[:, 3:4]
    scales = [mine[3:4]] + [one[3:4] for one in cols]

    def nugget(same):
        return jnp.where(same, NUGGET, 0.0)

    k_nuggets = [nugget(my_row == pivot)] + [nugget(tid == pivot) for tid in col_ids]
    f_nuggets = [nugget(tid == my_row) for tid in col_ids]
    r8 = lax.broadcasted_iota(jnp.int32, (ROWS, width), 0)
    l8 = lax.broadcasted_iota(jnp.int32, (ROWS, width), 1)

    def kernel_rows(ref, g, m, extra, scale, column):
        lo = g * ROWS
        value = matern(ref[lo:lo + ROWS, m * width:(m + 1) * width])
        value = value + jnp.where(l8 == r8 + lo, extra, 0.0)
        value = value * scale
        if column is not None:
            value = value * column[lo:lo + ROWS]
        ref[lo:lo + ROWS, m * width:(m + 1) * width] = value

    for g in range(width // ROWS):
        for m in range(parts + 1):
            kernel_rows(k_ref, g, m, k_nuggets[m], scales[m], None)
        for m in range(parts):
            kernel_rows(f_ref, g, m, f_nuggets[m], scales[m + 1], scale_r)
    half = width // 2

    def update(lo, final):
        row_high, row_low = split(x_ref[lo:lo + half, :width].T)
        for m in range(parts):
            high, lower = split(x_ref[lo:lo + half, (m + 1) * width:(m + 2) * width])
            product = dot(row_high, high, None) + (dot(row_high, lower, None) + dot(row_low, high, None))
            rest = f_ref[:, m * width:(m + 1) * width] - product
            if final:
                trail_ref[:, m, :] = rest.astype(jnp.bfloat16)
            else:
                f_ref[:, m * width:(m + 1) * width] = rest

    def done(lo, hi, left):
        x_ref[lo:hi, :] = dot(left, k_ref[:hi, :])
        if hi % half == 0:
            update(hi - half, hi == width)

    eliminate(t_ref, lambda: None, done)
    some = t_ref[pl.ds(pl.multiple_of(my_col * share, share), share), :]
    panel_ref[...] = dot(some, k_ref[:, :width])


def eliminate_panel(sites, panel, width, share, parts):
    return pl.pallas_call(
        body,
        out_shape=(
            jax.ShapeDtypeStruct((share, width), jnp.float32),
            jax.ShapeDtypeStruct((width, parts, width), jnp.bfloat16),
        ),
        in_specs=[pl.BlockSpec(memory_space=pltpu.SMEM), pl.BlockSpec(memory_space=pltpu.VMEM)],
        out_specs=[pl.BlockSpec(memory_space=pltpu.VMEM)] * 2,
        scratch_shapes=[
            pltpu.VMEM((width, width), jnp.float32),
            pltpu.VMEM((width, (parts + 1) * width), jnp.float32),
            pltpu.VMEM((width, parts * width), jnp.float32),
            pltpu.VMEM((width, (parts + 1) * width), jnp.float32),
        ],
        compiler_params=pltpu.CompilerParams(vmem_limit_bytes=48 << 20),
        name="eliminate_panel",
    )(panel, sites)


def on_device(site_cells, site_scale, panel):
    width = site_cells.shape[2]
    n_row, n_col = lax.axis_size("row"), lax.axis_size("col")
    sites = gather_sites(site_cells, site_scale, panel)
    panel_out, trailing = eliminate_panel(sites, panel, width, width // n_col, n_row // n_col)
    return panel_out.T[None], trailing[None]


def solution(mesh):
    placed = (P(None, None, "row"), P(None, "row"), P())
    return jax.shard_map(
        on_device,
        mesh=mesh,
        in_specs=placed,
        out_specs=(P(None, "row", "col"), P(None, "row", None, "col")),
        check_vma=False,
    )
```

```python
import math
import jax
import jax.numpy as jnp
from jax import lax
from jax.experimental import pallas as pl
from jax.experimental.pallas import tpu as pltpu
from jax.sharding import PartitionSpec as P

MESH = pl.DeviceIdType.MESH
NUGGET = 0.25
INV_LENGTH = 1.7320508075688772 / 12.0
LOG2E = 1.0 / math.log(2.0)
HI = lax.Precision.HIGHEST
PART = 128
HALF = 64
ROWS = 8
DEPTH = 4
ORDER = (2, 1, 3)


def dot(a, b, precision=HI):
    return jnp.dot(a, b, precision=precision, preferred_element_type=jnp.float32)


def dot_tn(a, b, precision=HI):
    return lax.dot_general(a, b, (((0,), (0,)), ((), ())), precision=precision, preferred_element_type=jnp.float32)


def split(a):
    high = a.astype(jnp.bfloat16)
    return high, (a - high.astype(jnp.float32)).astype(jnp.bfloat16)


def dot3(a, b):
    (ah, al), (bh, bl) = a, b
    return dot(ah, bh, None) + (dot(ah, bl, None) + dot(al, bh, None))


def dot3_tn(a, b):
    (ah, al), (bh, bl) = a, b
    return dot_tn(ah, bh, None) + (dot_tn(ah, bl, None) + dot_tn(al, bh, None))


def features(tile):
    x, y, z = tile[0:1], tile[1:2], 2.0 * tile[2:3]
    norm = x * x + y * y + z * z
    high = jnp.floor(norm * (1.0 / 256.0)) * 256.0
    low = norm - high
    one, zero = jnp.ones_like(x), jnp.zeros_like(x)
    left = jnp.concatenate([x, y, z, high, low, one, one, zero], axis=0)
    right = jnp.concatenate([-2.0 * x, -2.0 * y, -2.0 * z, one, one, high, low, zero], axis=0)
    return left, right


def squared(left, right):
    return dot_tn(left, right, lax.Precision.DEFAULT)


def matern(squares):
    radius = squares * lax.rsqrt(jnp.maximum(squares, 0.5)) * INV_LENGTH
    return (1.0 + radius) * jnp.exp2(radius * -LOG2E)


def col(x, k):
    return jnp.broadcast_to(x[:, k:k + 1], (ROWS, PART))


def row(x, j):
    return jnp.broadcast_to(x[j:j + 1, :], (ROWS, PART))


def inverse_factor(block):
    groups, half = PART // ROWS, HALF // ROWS
    sub = lax.broadcasted_iota(jnp.int32, (ROWS, PART), 0)
    lane = lax.broadcasted_iota(jnp.int32, (ROWS, PART), 1)
    t = [block(g) for g in range(groups)]
    out = []
    for base in range(0, groups, half):
        top = base + half
        raw = []
        c = [col(t[base], base * ROWS + k) for k in range(ROWS)]
        for p in range(base, top):
            lo = p * ROWS
            inside = jnp.logical_and(lane >= lo, lane < lo + ROWS)
            steps = []
            diag = jnp.ones((ROWS, PART), jnp.float32)
            own = jnp.where(inside, jnp.where(lane - lo == sub, 1.0, 0.0), t[p])
            last = p + 1 == top
            if not last:
                cc = [col(t[p + 1], lo + k) for k in range(ROWS)]
                cn = [col(t[p + 1], lo + ROWS + k) for k in range(ROWS)]
                tg = jnp.where(inside, 0.0, t[p + 1])
            for j in range(ROWS):
                d = row(c[j], j)
                diag = jnp.where(sub == j, d, diag)
                inv = 1.0 / d
                rc = [row(c[k], j) for k in range(j + 1, ROWS)]
                ra = row(own, j)
                steps.append((inv, rc, ra))
                if j < ROWS - 1:
                    m = jnp.where(sub > j, c[j] * inv, 0.0)
                    for k in range(j + 1, ROWS):
                        c[k] = c[k] - m * rc[k - j - 1]
                    own = own - m * ra
                if not last:
                    m = cc[j] * inv
                    for k in range(ROWS):
                        cn[k] = cn[k] - m * row(cc[j], k)
                    for k in range(j + 1, ROWS):
                        cc[k] = cc[k] - m * rc[k - j - 1]
                    tg = tg - m * ra
            raw.append(own * lax.rsqrt(diag))
            if last:
                break
            t[p + 1] = tg
            c = cn
            for g in range(p + 2, top):
                cc = [col(t[g], lo + k) for k in range(ROWS)]
                tg = jnp.where(inside, 0.0, t[g])
                for j in range(ROWS):
                    inv, rc, ra = steps[j]
                    m = cc[j] * inv
                    for k in range(j + 1, ROWS):
                        cc[k] = cc[k] - m * rc[k - j - 1]
                    tg = tg - m * ra
                t[g] = tg
        for i, r in enumerate(raw):
            out.append(jnp.where(lane < (base + i + 1) * ROWS, r, 0.0))
        if top < groups:
            done = top * ROWS
            u = jnp.concatenate(
                [jnp.where(jnp.logical_or(lane < (base + i + 1) * ROWS, lane >= done), r, 0.0) for i, r in enumerate(raw)],
                axis=0,
            )
            u = split(u)
            update = dot3_tn([v[:, done:] for v in u], u)
            for g in range(top, groups):
                keep = jnp.where(jnp.logical_and(lane >= base * ROWS, lane < done), 0.0, t[g])
                t[g] = keep - update[(g - top) * ROWS:(g - top + 1) * ROWS]
    return jnp.concatenate(out, axis=0)


def eliminate(t_ref, k_ref, u_refs, x_refs, done):
    n = t_ref.shape[0]
    for lo in range(0, n, PART):
        hi = lo + PART
        small = split(inverse_factor(lambda g: t_ref[lo + g * ROWS:lo + (g + 1) * ROWS, lo:hi]))
        if hi < n:
            after = hi + PART
            right = split(dot3(small, split(t_ref[lo:hi, hi:after])))
            t_ref[hi:after, hi:after] = t_ref[hi:after, hi:after] - dot3_tn(right, right)
            for ref, value in zip(u_refs, right):
                ref[lo:hi, hi:after] = value
            if after < n:
                far = split(dot3(small, split(t_ref[lo:hi, after:])))
                t_ref[hi:after, after:] = t_ref[hi:after, after:] - dot3_tn(right, far)
                t_ref[after:, after:] = t_ref[after:, after:] - dot3_tn(far, far)
                for ref, value in zip(u_refs, far):
                    ref[lo:hi, after:] = value
        for ref, value in zip(x_refs, split(dot3(small, split(k_ref[lo:hi, :])))):
            ref[lo:hi, :] = value
        if hi < n:
            k_ref[hi:after, :] = k_ref[hi:after, :] - dot3_tn(
                [ref[:hi, hi:after] for ref in u_refs], [ref[:hi, :] for ref in x_refs]
            )
        done(hi)


def place(n_line):
    my_row = lax.axis_index("row")
    core = lax.rem(my_row, 2)
    deep = lax.rem(lax.div(my_row, 2), n_line)
    flat = lax.div(my_row, 2 * n_line) * 2 + core
    return deep, flat


def row_of(flat, deep, n_line):
    return lax.div(flat, 2) * (2 * n_line) + deep * 2 + lax.rem(flat, 2)


def gather_body(p_ref, cells_ref, scale_ref, out_ref, cells_line, scale_line, picks, mine, line_send, line_recv, plane_send, plane_recv, own_sem):
    n_line, n_plane = cells_line.shape[0], out_ref.shape[0] - 1
    deep, flat = place(n_line)
    my_col = lax.axis_index("col")
    block = lax.div(my_col, n_line) * n_line
    crossed = block + lax.rem(my_col - block + n_line // 2, n_line)

    def ahead(k):
        there = {"row": row_of(flat, lax.rem(deep + k, n_line), n_line)}
        if 2 * k == n_line:
            there["col"] = crossed
        return there

    def aside(k):
        return {"row": row_of(lax.rem(flat + k, n_plane), deep, n_line)}

    barrier = pltpu.get_barrier_semaphore()
    for k in range(1, n_line):
        pl.semaphore_signal(barrier, inc=1, device_id=ahead(k), device_id_type=MESH)
    for k in range(1, n_plane):
        pl.semaphore_signal(barrier, inc=1, device_id=aside(k), device_id_type=MESH)
    own = [
        pltpu.make_async_copy(cells_ref, cells_line.at[0], own_sem.at[0]),
        pltpu.make_async_copy(scale_ref, scale_line.at[0], own_sem.at[1]),
    ]
    for copy in own:
        copy.start()
    pl.semaphore_wait(barrier, n_line + n_plane - 2)

    line = []
    for k in ORDER:
        for i, (src, dst) in enumerate(((cells_ref, cells_line), (scale_ref, scale_line))):
            copy = pltpu.make_async_remote_copy(
                src_ref=src, dst_ref=dst.at[k],
                send_sem=line_send.at[k, i], recv_sem=line_recv.at[k, i],
                device_id=ahead(k), device_id_type=MESH,
            )
            copy.start()
            line.append(copy)
    for copy in own:
        copy.wait()
    for axis in range(3):
        mine[0, axis:axis + 1] = cells_line[0, axis].astype(jnp.float32)
    mine[0, 3:4] = scale_line[0]
    mine[1] = mine[0]
    keep = pltpu.make_async_copy(mine, out_ref.at[n_plane], own_sem.at[2])
    keep.start()
    for copy in line:
        copy.wait()
    pivot = p_ref[0]
    col_deep = lax.rem(lax.div(my_col, 2), n_line)
    for axis in range(4):
        chosen = jnp.zeros((1, mine.shape[2]), jnp.float32)
        column = chosen
        for k in range(n_line):
            deep_at = lax.rem(deep + n_line - k, n_line)
            held = cells_line[k, axis].astype(jnp.float32) if axis < 3 else scale_line[k]
            chosen = jnp.where(row_of(flat, deep_at, n_line) == pivot, held, chosen)
            column = jnp.where(deep_at == col_deep, held, column)
        picks[0, axis:axis + 1] = chosen
        picks[1, axis:axis + 1] = column
    plane = []
    for k in range(1, n_plane):
        copy = pltpu.make_async_remote_copy(
            src_ref=picks, dst_ref=out_ref.at[k],
            send_sem=plane_send.at[k], recv_sem=plane_recv.at[k],
            device_id=aside(k), device_id_type=MESH,
        )
        copy.start()
        plane.append(copy)
    last = pltpu.make_async_copy(picks, out_ref.at[0], own_sem.at[3])
    last.start()
    keep.wait()
    last.wait()
    for copy in plane:
        copy.wait()


def gather_sites(cells, scale, panel):
    width = cells.shape[2]
    n_plane = lax.axis_size("row") // DEPTH
    return pl.pallas_call(
        gather_body,
        out_shape=jax.ShapeDtypeStruct((n_plane + 1, 2, 4, width), jnp.float32),
        in_specs=[pl.BlockSpec(memory_space=pltpu.SMEM)] + [pl.BlockSpec(memory_space=pltpu.HBM)] * 2,
        out_specs=pl.BlockSpec(memory_space=pltpu.HBM),
        scratch_shapes=[
            pltpu.VMEM((DEPTH, 3, 1, width), jnp.int32),
            pltpu.VMEM((DEPTH, 1, width), jnp.float32),
            pltpu.VMEM((2, 4, width), jnp.float32),
            pltpu.VMEM((2, 4, width), jnp.float32),
            pltpu.SemaphoreType.DMA((DEPTH, 2)),
            pltpu.SemaphoreType.DMA((DEPTH, 2)),
            pltpu.SemaphoreType.DMA((n_plane,)),
            pltpu.SemaphoreType.DMA((n_plane,)),
            pltpu.SemaphoreType.DMA((4,)),
        ],
        compiler_params=pltpu.CompilerParams(collective_id=0, has_side_effects=True),
        name="gather_sites",
    )(panel, cells, scale)


def pick(sites_ref, parts):
    n_plane = sites_ref.shape[0] - 1
    deep, flat = place(DEPTH)
    my_col, n_col = lax.axis_index("col"), lax.axis_size("col")
    pivot = sites_ref[0, 0]
    for k in range(1, n_plane):
        pivot = pivot + sites_ref[k, 0]
    cols = []
    for m in range(parts):
        tile = my_col + m * n_col
        home = lax.div(tile, 2 * DEPTH) * 2 + lax.rem(tile, 2)
        held = sites_ref[0, 1]
        for k in range(1, n_plane):
            held = jnp.where(lax.rem(flat + n_plane - k, n_plane) == home, sites_ref[k, 1], held)
        cols.append(held)
    return pivot, sites_ref[n_plane, 0], cols


def body(p_ref, sites_ref, panel_ref, trail_ref, t_ref, k_ref, f_ref, u_high, u_low, x_high, x_low):
    share, width = panel_ref.shape
    parts = trail_ref.shape[1]
    my_row = lax.axis_index("row")
    my_col = lax.axis_index("col")
    n_col = lax.axis_size("col")
    pivot = p_ref[0]
    piv, mine, cols = pick(sites_ref, parts)
    col_ids = [my_col + m * n_col for m in range(parts)]
    piv_left, piv_right = features(piv)
    my_left, my_right = features(mine)
    rights = [my_right] + [features(one)[1] for one in cols]
    sub = lax.broadcasted_iota(jnp.int32, (width, width), 0)
    lane = lax.broadcasted_iota(jnp.int32, (width, width), 1)
    t_ref[...] = matern(squared(piv_left, piv_right)) + jnp.where(sub == lane, NUGGET, 0.0)
    for m, right in enumerate(rights):
        k_ref[:, m * width:(m + 1) * width] = squared(piv_left, right)
        if m:
            f_ref[:, (m - 1) * width:m * width] = squared(my_left, right)
    scale_r = mine.T[:, 3:4]
    scales = [mine[3:4]] + [one[3:4] for one in cols]

    def nugget(same):
        return jnp.where(same, NUGGET, 0.0)

    k_nuggets = [nugget(my_row == pivot)] + [nugget(tid == pivot) for tid in col_ids]
    f_nuggets = [nugget(tid == my_row) for tid in col_ids]
    r8 = lax.broadcasted_iota(jnp.int32, (ROWS, width), 0)
    l8 = lax.broadcasted_iota(jnp.int32, (ROWS, width), 1)

    def kernel_rows(ref, g, m, extra, scale, column):
        lo = g * ROWS
        value = matern(ref[lo:lo + ROWS, m * width:(m + 1) * width])
        value = value + jnp.where(l8 == r8 + lo, extra, 0.0)
        value = value * scale
        if column is not None:
            value = value * column[lo:lo + ROWS]
        ref[lo:lo + ROWS, m * width:(m + 1) * width] = value

    for g in range(width // ROWS):
        for m in range(parts + 1):
            kernel_rows(k_ref, g, m, k_nuggets[m], scales[m], None)
        for m in range(parts):
            kernel_rows(f_ref, g, m, f_nuggets[m], scales[m + 1], scale_r)
    half = width // 2

    def update(lo, final):
        rows = [ref[lo:lo + half, :width] for ref in (x_high, x_low)]
        for m in range(parts):
            rest = f_ref[:, m * width:(m + 1) * width] - dot3_tn(
                rows, [ref[lo:lo + half, (m + 1) * width:(m + 2) * width] for ref in (x_high, x_low)]
            )
            if final:
                trail_ref[:, m, :] = rest.astype(jnp.bfloat16)
            else:
                f_ref[:, m * width:(m + 1) * width] = rest

    def done(hi):
        if hi % half == 0:
            update(hi - half, hi == width)

    eliminate(t_ref, k_ref, (u_high, u_low), (x_high, x_low), done)
    mine_rows = pl.ds(pl.multiple_of(my_col * share, share), share)
    panel_ref[...] = x_high[mine_rows, :width].astype(jnp.float32) + x_low[mine_rows, :width].astype(jnp.float32)


def eliminate_panel(sites, panel, width, share, parts):
    return pl.pallas_call(
        body,
        out_shape=(
            jax.ShapeDtypeStruct((share, width), jnp.float32),
            jax.ShapeDtypeStruct((width, parts, width), jnp.bfloat16),
        ),
        in_specs=[pl.BlockSpec(memory_space=pltpu.SMEM), pl.BlockSpec(memory_space=pltpu.VMEM)],
        out_specs=[pl.BlockSpec(memory_space=pltpu.VMEM)] * 2,
        scratch_shapes=[
            pltpu.VMEM((width, width), jnp.float32),
            pltpu.VMEM((width, (parts + 1) * width), jnp.float32),
            pltpu.VMEM((width, parts * width), jnp.float32),
            pltpu.VMEM((width, width), jnp.bfloat16),
            pltpu.VMEM((width, width), jnp.bfloat16),
            pltpu.VMEM((width, (parts + 1) * width), jnp.bfloat16),
            pltpu.VMEM((width, (parts + 1) * width), jnp.bfloat16),
        ],
        compiler_params=pltpu.CompilerParams(vmem_limit_bytes=48 << 20),
        name="eliminate_panel",
    )(panel, sites)


def on_device(site_cells, site_scale, panel):
    width = site_cells.shape[2]
    n_row, n_col = lax.axis_size("row"), lax.axis_size("col")
    sites = gather_sites(site_cells, site_scale, panel)
    panel_out, trailing = eliminate_panel(sites, panel, width, width // n_col, n_row // n_col)
    return panel_out.T[None], trailing[None]


def solution(mesh):
    placed = (P(None, None, "row"), P(None, "row"), P())
    return jax.shard_map(
        on_device,
        mesh=mesh,
        in_specs=placed,
        out_specs=(P(None, "row", "col"), P(None, "row", None, "col")),
        check_vma=False,
    )
```

```python
import math
import jax
import jax.numpy as jnp
from jax import lax
from jax.experimental import pallas as pl
from jax.experimental.pallas import tpu as pltpu
from jax.sharding import PartitionSpec as P

MESH = pl.DeviceIdType.MESH
NUGGET = 0.25
INV_LENGTH = 1.7320508075688772 / 12.0
LOG2E = 1.0 / math.log(2.0)
HI = lax.Precision.HIGHEST
PART = 128
HALF = 64
ROWS = 8
DEPTH = 4
ORDER = (2, 1, 3)


def dot(a, b, precision=HI):
    return jnp.dot(a, b, precision=precision, preferred_element_type=jnp.float32)


def dot_tn(a, b, precision=HI):
    return lax.dot_general(a, b, (((0,), (0,)), ((), ())), precision=precision, preferred_element_type=jnp.float32)


def split(a):
    high = a.astype(jnp.bfloat16)
    return high, (a - high.astype(jnp.float32)).astype(jnp.bfloat16)


def dot3(a, b):
    (ah, al), (bh, bl) = a, b
    if bh.shape[0] <= PART:
        return dot(jnp.concatenate([ah, al], axis=1), jnp.concatenate([bh, bh], axis=0), None) + dot(ah, bl, None)
    return dot(ah, bh, None) + (dot(ah, bl, None) + dot(al, bh, None))


def dot3_tn(a, b):
    (ah, al), (bh, bl) = a, b
    if bh.shape[0] <= PART:
        return dot_tn(jnp.concatenate([ah, al], axis=0), jnp.concatenate([bh, bh], axis=0), None) + dot_tn(ah, bl, None)
    return dot_tn(ah, bh, None) + (dot_tn(ah, bl, None) + dot_tn(al, bh, None))


def features(tile):
    x, y, z = tile[0:1], tile[1:2], 2.0 * tile[2:3]
    norm = x * x + y * y + z * z
    high = jnp.floor(norm * (1.0 / 256.0)) * 256.0
    low = norm - high
    one, zero = jnp.ones_like(x), jnp.zeros_like(x)
    left = jnp.concatenate([x, y, z, high, low, one, one, zero], axis=0)
    right = jnp.concatenate([-2.0 * x, -2.0 * y, -2.0 * z, one, one, high, low, zero], axis=0)
    return left, right


def squared(left, right):
    return dot_tn(left, right, lax.Precision.DEFAULT)


def matern(squares):
    radius = squares * lax.rsqrt(jnp.maximum(squares, 0.5)) * INV_LENGTH
    return (1.0 + radius) * jnp.exp2(radius * -LOG2E)


def col(x, k):
    return jnp.broadcast_to(x[:, k:k + 1], (ROWS, PART))


def row(x, j):
    return jnp.broadcast_to(x[j:j + 1, :], (ROWS, PART))


def inverse_factor(block):
    groups, half = PART // ROWS, HALF // ROWS
    sub = lax.broadcasted_iota(jnp.int32, (ROWS, PART), 0)
    lane = lax.broadcasted_iota(jnp.int32, (ROWS, PART), 1)
    t = [block(g) for g in range(groups)]
    out = []
    for base in range(0, groups, half):
        top = base + half
        raw = []
        c = [col(t[base], base * ROWS + k) for k in range(ROWS)]
        for p in range(base, top):
            lo = p * ROWS
            inside = jnp.logical_and(lane >= lo, lane < lo + ROWS)
            steps = []
            diag = jnp.ones((ROWS, PART), jnp.float32)
            own = jnp.where(inside, jnp.where(lane - lo == sub, 1.0, 0.0), t[p])
            last = p + 1 == top
            if not last:
                cc = [col(t[p + 1], lo + k) for k in range(ROWS)]
                cn = [col(t[p + 1], lo + ROWS + k) for k in range(ROWS)]
                tg = jnp.where(inside, 0.0, t[p + 1])
            for j in range(ROWS):
                d = row(c[j], j)
                diag = jnp.where(sub == j, d, diag)
                inv = 1.0 / d
                rc = [row(c[k], j) for k in range(j + 1, ROWS)]
                ra = row(own, j)
                steps.append((inv, rc, ra))
                if j < ROWS - 1:
                    m = jnp.where(sub > j, c[j] * inv, 0.0)
                    for k in range(j + 1, ROWS):
                        c[k] = c[k] - m * rc[k - j - 1]
                    own = own - m * ra
                if not last:
                    m = cc[j] * inv
                    for k in range(ROWS):
                        cn[k] = cn[k] - m * row(cc[j], k)
                    for k in range(j + 1, ROWS):
                        cc[k] = cc[k] - m * rc[k - j - 1]
                    tg = tg - m * ra
            raw.append(own * lax.rsqrt(diag))
            if last:
                break
            t[p + 1] = tg
            c = cn
            for g in range(p + 2, top):
                cc = [col(t[g], lo + k) for k in range(ROWS)]
                tg = jnp.where(inside, 0.0, t[g])
                for j in range(ROWS):
                    inv, rc, ra = steps[j]
                    m = cc[j] * inv
                    for k in range(j + 1, ROWS):
                        cc[k] = cc[k] - m * rc[k - j - 1]
                    tg = tg - m * ra
                t[g] = tg
        for i, r in enumerate(raw):
            out.append(jnp.where(lane < (base + i + 1) * ROWS, r, 0.0))
        if top < groups:
            done = top * ROWS
            u = jnp.concatenate(
                [jnp.where(jnp.logical_or(lane < (base + i + 1) * ROWS, lane >= done), r, 0.0) for i, r in enumerate(raw)],
                axis=0,
            )
            u = split(u)
            update = dot3_tn([v[:, done:] for v in u], u)
            for g in range(top, groups):
                keep = jnp.where(jnp.logical_and(lane >= base * ROWS, lane < done), 0.0, t[g])
                t[g] = keep - update[(g - top) * ROWS:(g - top + 1) * ROWS]
    return jnp.concatenate(out, axis=0)


def eliminate(t_ref, k_ref, u_refs, x_refs, done):
    n = t_ref.shape[0]
    for lo in range(0, n, PART):
        hi = lo + PART
        small = split(inverse_factor(lambda g: t_ref[lo + g * ROWS:lo + (g + 1) * ROWS, lo:hi]))
        if hi < n:
            after = hi + PART
            right = split(dot3(small, split(t_ref[lo:hi, hi:after])))
            t_ref[hi:after, hi:after] = t_ref[hi:after, hi:after] - dot3_tn(right, right)
            for ref, value in zip(u_refs, right):
                ref[lo:hi, hi:after] = value
            if after < n:
                far = split(dot3(small, split(t_ref[lo:hi, after:])))
                t_ref[hi:after, after:] = t_ref[hi:after, after:] - dot3_tn(right, far)
                t_ref[after:, after:] = t_ref[after:, after:] - dot3_tn(far, far)
                for ref, value in zip(u_refs, far):
                    ref[lo:hi, after:] = value
        for ref, value in zip(x_refs, split(dot3(small, split(k_ref[lo:hi, :])))):
            ref[lo:hi, :] = value
        if hi < n:
            k_ref[hi:after, :] = k_ref[hi:after, :] - dot3_tn(
                [ref[:hi, hi:after] for ref in u_refs], [ref[:hi, :] for ref in x_refs]
            )
        done(hi)


def place(n_line):
    my_row = lax.axis_index("row")
    core = lax.rem(my_row, 2)
    deep = lax.rem(lax.div(my_row, 2), n_line)
    flat = lax.div(my_row, 2 * n_line) * 2 + core
    return deep, flat


def row_of(flat, deep, n_line):
    return lax.div(flat, 2) * (2 * n_line) + deep * 2 + lax.rem(flat, 2)


def gather_body(p_ref, cells_ref, scale_ref, out_ref, cells_line, scale_line, picks, mine, line_send, line_recv, plane_send, plane_recv, own_sem):
    n_line, n_plane = cells_line.shape[0], out_ref.shape[0] - 1
    deep, flat = place(n_line)
    my_col = lax.axis_index("col")
    block = lax.div(my_col, n_line) * n_line
    crossed = block + lax.rem(my_col - block + n_line // 2, n_line)

    def ahead(k):
        there = {"row": row_of(flat, lax.rem(deep + k, n_line), n_line)}
        if 2 * k == n_line:
            there["col"] = crossed
        return there

    def aside(k):
        return {"row": row_of(lax.rem(flat + k, n_plane), deep, n_line)}

    barrier = pltpu.get_barrier_semaphore()
    for k in range(1, n_line):
        pl.semaphore_signal(barrier, inc=1, device_id=ahead(k), device_id_type=MESH)
    for k in range(1, n_plane):
        pl.semaphore_signal(barrier, inc=1, device_id=aside(k), device_id_type=MESH)
    own = [
        pltpu.make_async_copy(cells_ref, cells_line.at[0], own_sem.at[0]),
        pltpu.make_async_copy(scale_ref, scale_line.at[0], own_sem.at[1]),
    ]
    for copy in own:
        copy.start()
    pl.semaphore_wait(barrier, n_line + n_plane - 2)

    line = []
    for k in ORDER:
        for i, (src, dst) in enumerate(((cells_ref, cells_line), (scale_ref, scale_line))):
            copy = pltpu.make_async_remote_copy(
                src_ref=src, dst_ref=dst.at[k],
                send_sem=line_send.at[k, i], recv_sem=line_recv.at[k, i],
                device_id=ahead(k), device_id_type=MESH,
            )
            copy.start()
            line.append(copy)
    for copy in own:
        copy.wait()
    for axis in range(3):
        mine[0, axis:axis + 1] = cells_line[0, axis].astype(jnp.float32)
    mine[0, 3:4] = scale_line[0]
    mine[1] = mine[0]
    keep = pltpu.make_async_copy(mine, out_ref.at[n_plane], own_sem.at[2])
    keep.start()
    for copy in line:
        copy.wait()
    pivot = p_ref[0]
    col_deep = lax.rem(lax.div(my_col, 2), n_line)
    for axis in range(4):
        chosen = jnp.zeros((1, mine.shape[2]), jnp.float32)
        column = chosen
        for k in range(n_line):
            deep_at = lax.rem(deep + n_line - k, n_line)
            held = cells_line[k, axis].astype(jnp.float32) if axis < 3 else scale_line[k]
            chosen = jnp.where(row_of(flat, deep_at, n_line) == pivot, held, chosen)
            column = jnp.where(deep_at == col_deep, held, column)
        picks[0, axis:axis + 1] = chosen
        picks[1, axis:axis + 1] = column
    plane = []
    for k in (7, 6, 5, 4, 3, 2, 1):
        copy = pltpu.make_async_remote_copy(
            src_ref=picks, dst_ref=out_ref.at[k],
            send_sem=plane_send.at[k], recv_sem=plane_recv.at[k],
            device_id=aside(k), device_id_type=MESH,
        )
        copy.start()
        plane.append(copy)
    last = pltpu.make_async_copy(picks, out_ref.at[0], own_sem.at[3])
    last.start()
    keep.wait()
    last.wait()
    for copy in plane:
        copy.wait()


def gather_sites(cells, scale, panel):
    width = cells.shape[2]
    n_plane = lax.axis_size("row") // DEPTH
    return pl.pallas_call(
        gather_body,
        out_shape=jax.ShapeDtypeStruct((n_plane + 1, 2, 4, width), jnp.float32),
        in_specs=[pl.BlockSpec(memory_space=pltpu.SMEM)] + [pl.BlockSpec(memory_space=pltpu.HBM)] * 2,
        out_specs=pl.BlockSpec(memory_space=pltpu.HBM),
        scratch_shapes=[
            pltpu.VMEM((DEPTH, 3, 1, width), jnp.int32),
            pltpu.VMEM((DEPTH, 1, width), jnp.float32),
            pltpu.VMEM((2, 4, width), jnp.float32),
            pltpu.VMEM((2, 4, width), jnp.float32),
            pltpu.SemaphoreType.DMA((DEPTH, 2)),
            pltpu.SemaphoreType.DMA((DEPTH, 2)),
            pltpu.SemaphoreType.DMA((n_plane,)),
            pltpu.SemaphoreType.DMA((n_plane,)),
            pltpu.SemaphoreType.DMA((4,)),
        ],
        compiler_params=pltpu.CompilerParams(collective_id=0, has_side_effects=True),
        name="gather_sites",
    )(panel, cells, scale)


def pick(sites_ref, parts):
    n_plane = sites_ref.shape[0] - 1
    deep, flat = place(DEPTH)
    my_col, n_col = lax.axis_index("col"), lax.axis_size("col")
    pivot = sites_ref[0, 0]
    for k in range(1, n_plane):
        pivot = pivot + sites_ref[k, 0]
    cols = []
    for m in range(parts):
        tile = my_col + m * n_col
        home = lax.div(tile, 2 * DEPTH) * 2 + lax.rem(tile, 2)
        held = sites_ref[0, 1]
        for k in range(1, n_plane):
            held = jnp.where(lax.rem(flat + n_plane - k, n_plane) == home, sites_ref[k, 1], held)
        cols.append(held)
    return pivot, sites_ref[n_plane, 0], cols


def body(p_ref, sites_ref, panel_ref, trail_ref, t_ref, k_ref, f_ref, u_high, u_low, x_high, x_low):
    share, width = panel_ref.shape
    parts = trail_ref.shape[1]
    my_row = lax.axis_index("row")
    my_col = lax.axis_index("col")
    n_col = lax.axis_size("col")
    pivot = p_ref[0]
    piv, mine, cols = pick(sites_ref, parts)
    col_ids = [my_col + m * n_col for m in range(parts)]
    piv_left, piv_right = features(piv)
    my_left, my_right = features(mine)
    rights = [my_right] + [features(one)[1] for one in cols]
    sub = lax.broadcasted_iota(jnp.int32, (width, width), 0)
    lane = lax.broadcasted_iota(jnp.int32, (width, width), 1)
    t_ref[...] = matern(squared(piv_left, piv_right)) + jnp.where(sub == lane, NUGGET, 0.0)
    for m, right in enumerate(rights):
        k_ref[:, m * width:(m + 1) * width] = squared(piv_left, right)
        if m:
            f_ref[:, (m - 1) * width:m * width] = squared(my_left, right)
    scale_r = mine.T[:, 3:4]
    scales = [mine[3:4]] + [one[3:4] for one in cols]

    slopes = [one * INV_LENGTH for one in scales]

    def nugget(same):
        return jnp.where(same, NUGGET, 0.0)

    k_nuggets = [nugget(my_row == pivot)] + [nugget(tid == pivot) for tid in col_ids]
    f_nuggets = [nugget(tid == my_row) for tid in col_ids]
    r8 = lax.broadcasted_iota(jnp.int32, (ROWS, PART), 0)
    l8 = lax.broadcasted_iota(jnp.int32, (ROWS, PART), 1)

    def kernel_rows(ref, g, m, extra, scale, slope, column):
        lo = g * ROWS
        at = lo // PART * PART
        squares = ref[lo:lo + ROWS, m * width:(m + 1) * width]
        length = squares * lax.rsqrt(jnp.maximum(squares, 0.5))
        value = (scale + slope * length) * jnp.exp2(length * (-LOG2E * INV_LENGTH))
        if column is not None:
            value = value * column[lo:lo + ROWS]
        ref[lo:lo + ROWS, m * width:(m + 1) * width] = value
        near = scale[:, at:at + PART] * extra
        if column is not None:
            near = near * column[lo:lo + ROWS]
        spot = ref.at[lo:lo + ROWS, m * width + at:m * width + at + PART]
        spot[...] = value[:, at:at + PART] + jnp.where(l8 == r8 + (lo - at), near, 0.0)

    for g in range(width // ROWS):
        for m in range(parts + 1):
            kernel_rows(k_ref, g, m, k_nuggets[m], scales[m], slopes[m], None)
        for m in range(parts):
            kernel_rows(f_ref, g, m, f_nuggets[m], scales[m + 1], slopes[m + 1], scale_r)
    half = width // 2

    def update(lo, final):
        rows = [ref[lo:lo + half, :width] for ref in (x_high, x_low)]
        for m in range(parts):
            rest = f_ref[:, m * width:(m + 1) * width] - dot3_tn(
                rows, [ref[lo:lo + half, (m + 1) * width:(m + 2) * width] for ref in (x_high, x_low)]
            )
            if final:
                trail_ref[:, m, :] = rest.astype(jnp.bfloat16)
            else:
                f_ref[:, m * width:(m + 1) * width] = rest

    def done(hi):
        if hi % half == 0:
            update(hi - half, hi == width)

    eliminate(t_ref, k_ref, (u_high, u_low), (x_high, x_low), done)
    mine_rows = pl.ds(pl.multiple_of(my_col * share, share), share)
    panel_ref[...] = x_high[mine_rows, :width].astype(jnp.float32) + x_low[mine_rows, :width].astype(jnp.float32)


def eliminate_panel(sites, panel, width, share, parts):
    return pl.pallas_call(
        body,
        out_shape=(
            jax.ShapeDtypeStruct((share, width), jnp.float32),
            jax.ShapeDtypeStruct((width, parts, width), jnp.bfloat16),
        ),
        in_specs=[pl.BlockSpec(memory_space=pltpu.SMEM), pl.BlockSpec(memory_space=pltpu.VMEM)],
        out_specs=[pl.BlockSpec(memory_space=pltpu.VMEM)] * 2,
        scratch_shapes=[
            pltpu.VMEM((width, width), jnp.float32),
            pltpu.VMEM((width, (parts + 1) * width), jnp.float32),
            pltpu.VMEM((width, parts * width), jnp.float32),
            pltpu.VMEM((width, width), jnp.bfloat16),
            pltpu.VMEM((width, width), jnp.bfloat16),
            pltpu.VMEM((width, (parts + 1) * width), jnp.bfloat16),
            pltpu.VMEM((width, (parts + 1) * width), jnp.bfloat16),
        ],
        compiler_params=pltpu.CompilerParams(vmem_limit_bytes=48 << 20),
        name="eliminate_panel",
    )(panel, sites)


def on_device(site_cells, site_scale, panel):
    width = site_cells.shape[2]
    n_row, n_col = lax.axis_size("row"), lax.axis_size("col")
    sites = gather_sites(site_cells, site_scale, panel)
    panel_out, trailing = eliminate_panel(sites, panel, width, width // n_col, n_row // n_col)
    return panel_out.T[None], trailing[None]


def solution(mesh):
    placed = (P(None, None, "row"), P(None, "row"), P())
    return jax.shard_map(
        on_device,
        mesh=mesh,
        in_specs=placed,
        out_specs=(P(None, "row", "col"), P(None, "row", None, "col")),
        check_vma=False,
    )
```

```python
import math
import jax
import jax.numpy as jnp
from jax import lax
from jax.experimental import pallas as pl
from jax.experimental.pallas import tpu as pltpu
from jax.sharding import PartitionSpec as P

MESH = pl.DeviceIdType.MESH
NUGGET = 0.25
INV_LENGTH = 1.7320508075688772 / 12.0
LOG2E = 1.0 / math.log(2.0)
HI = lax.Precision.HIGHEST
PART = 128
HALF = 64
ROWS = 8
DEPTH = 4
ORDER = (2, 1, 3)


def dot(a, b, precision=HI):
    return jnp.dot(a, b, precision=precision, preferred_element_type=jnp.float32)


def dot_tn(a, b, precision=HI):
    return lax.dot_general(a, b, (((0,), (0,)), ((), ())), precision=precision, preferred_element_type=jnp.float32)


def split(a):
    high = a.astype(jnp.bfloat16)
    return high, (a - high.astype(jnp.float32)).astype(jnp.bfloat16)


def dot3(a, b):
    (ah, al), (bh, bl) = a, b
    if bh.shape[0] <= PART:
        return dot(jnp.concatenate([ah, al], axis=1), jnp.concatenate([bh, bh], axis=0), None) + dot(ah, bl, None)
    return dot(ah, bh, None) + (dot(ah, bl, None) + dot(al, bh, None))


def dot3_tn(a, b):
    (ah, al), (bh, bl) = a, b
    if bh.shape[0] <= PART:
        return dot_tn(jnp.concatenate([ah, al], axis=0), jnp.concatenate([bh, bh], axis=0), None) + dot_tn(ah, bl, None)
    return dot_tn(ah, bh, None) + (dot_tn(ah, bl, None) + dot_tn(al, bh, None))


def features(tile):
    x, y, z = tile[0:1], tile[1:2], 2.0 * tile[2:3]
    norm = x * x + y * y + z * z
    high = jnp.floor(norm * (1.0 / 256.0)) * 256.0
    low = norm - high
    one, zero = jnp.ones_like(x), jnp.zeros_like(x)
    left = jnp.concatenate([x, y, z, high, low, one, one, zero], axis=0)
    right = jnp.concatenate([-2.0 * x, -2.0 * y, -2.0 * z, one, one, high, low, zero], axis=0)
    return left, right


def squared(left, right):
    return dot_tn(left, right, lax.Precision.DEFAULT)


def matern(squares):
    radius = squares * lax.rsqrt(jnp.maximum(squares, 0.5)) * INV_LENGTH
    return (1.0 + radius) * jnp.exp2(radius * -LOG2E)


def col(x, k):
    return jnp.broadcast_to(x[:, k:k + 1], (ROWS, PART))


def row(x, j):
    return jnp.broadcast_to(x[j:j + 1, :], (ROWS, PART))


def inverse_factor(block):
    groups, half = PART // ROWS, HALF // ROWS
    sub = lax.broadcasted_iota(jnp.int32, (ROWS, PART), 0)
    lane = lax.broadcasted_iota(jnp.int32, (ROWS, PART), 1)
    t = [block(g) for g in range(groups)]
    out = []
    for base in range(0, groups, half):
        top = base + half
        raw = []
        c = [col(t[base], base * ROWS + k) for k in range(ROWS)]
        for p in range(base, top):
            lo = p * ROWS
            inside = jnp.logical_and(lane >= lo, lane < lo + ROWS)
            steps = []
            diag = jnp.ones((ROWS, PART), jnp.float32)
            own = jnp.where(inside, jnp.where(lane - lo == sub, 1.0, 0.0), t[p])
            last = p + 1 == top
            if not last:
                cc = [col(t[p + 1], lo + k) for k in range(ROWS)]
                cn = [col(t[p + 1], lo + ROWS + k) for k in range(ROWS)]
                tg = jnp.where(inside, 0.0, t[p + 1])
            for j in range(ROWS):
                d = row(c[j], j)
                diag = jnp.where(sub == j, d, diag)
                inv = 1.0 / d
                rc = [row(c[k], j) for k in range(j + 1, ROWS)]
                ra = row(own, j)
                steps.append((inv, rc, ra))
                if j < ROWS - 1:
                    m = jnp.where(sub > j, c[j] * inv, 0.0)
                    for k in range(j + 1, ROWS):
                        c[k] = c[k] - m * rc[k - j - 1]
                    own = own - m * ra
                if not last:
                    m = cc[j] * inv
                    for k in range(ROWS):
                        cn[k] = cn[k] - m * row(cc[j], k)
                    for k in range(j + 1, ROWS):
                        cc[k] = cc[k] - m * rc[k - j - 1]
                    tg = tg - m * ra
            raw.append(own * lax.rsqrt(diag))
            if last:
                break
            t[p + 1] = tg
            c = cn
            for g in range(p + 2, top):
                cc = [col(t[g], lo + k) for k in range(ROWS)]
                tg = jnp.where(inside, 0.0, t[g])
                for j in range(ROWS):
                    inv, rc, ra = steps[j]
                    m = cc[j] * inv
                    for k in range(j + 1, ROWS):
                        cc[k] = cc[k] - m * rc[k - j - 1]
                    tg = tg - m * ra
                t[g] = tg
        for i, r in enumerate(raw):
            out.append(jnp.where(lane < (base + i + 1) * ROWS, r, 0.0))
        if top < groups:
            done = top * ROWS
            u = jnp.concatenate(
                [jnp.where(jnp.logical_or(lane < (base + i + 1) * ROWS, lane >= done), r, 0.0) for i, r in enumerate(raw)],
                axis=0,
            )
            u = split(u)
            update = dot3_tn([v[:, done:] for v in u], u)
            for g in range(top, groups):
                keep = jnp.where(jnp.logical_and(lane >= base * ROWS, lane < done), 0.0, t[g])
                t[g] = keep - update[(g - top) * ROWS:(g - top + 1) * ROWS]
    return jnp.concatenate(out, axis=0)


def eliminate(t_ref, k_ref, u_refs, x_refs, done):
    n = t_ref.shape[0]
    for lo in range(0, n, PART):
        hi = lo + PART
        small = split(inverse_factor(lambda g: t_ref[lo + g * ROWS:lo + (g + 1) * ROWS, lo:hi]))
        if hi < n:
            after = hi + PART
            right = split(dot3(small, split(t_ref[lo:hi, hi:after])))
            t_ref[hi:after, hi:after] = t_ref[hi:after, hi:after] - dot3_tn(right, right)
            for ref, value in zip(u_refs, right):
                ref[lo:hi, hi:after] = value
            if after < n:
                far = split(dot3(small, split(t_ref[lo:hi, after:])))
                t_ref[hi:after, after:] = t_ref[hi:after, after:] - dot3_tn(right, far)
                t_ref[after:, after:] = t_ref[after:, after:] - dot3_tn(far, far)
                for ref, value in zip(u_refs, far):
                    ref[lo:hi, after:] = value
        for ref, value in zip(x_refs, split(dot3(small, split(k_ref[lo:hi, :])))):
            ref[lo:hi, :] = value
        if hi < n:
            k_ref[hi:after, :] = k_ref[hi:after, :] - dot3_tn(
                [ref[:hi, hi:after] for ref in u_refs], [ref[:hi, :] for ref in x_refs]
            )
        done(hi)


def place(n_line):
    my_row = lax.axis_index("row")
    core = lax.rem(my_row, 2)
    deep = lax.rem(lax.div(my_row, 2), n_line)
    flat = lax.div(my_row, 2 * n_line) * 2 + core
    return deep, flat


def row_of(flat, deep, n_line):
    return lax.div(flat, 2) * (2 * n_line) + deep * 2 + lax.rem(flat, 2)


def gather_body(p_ref, cells_ref, scale_ref, out_ref, cells, scale, tiles, picks, line_send, line_recv, plane_send, plane_recv, own_sem):
    n_line, n_plane = tiles.shape[0], out_ref.shape[0] - 1
    deep, flat = place(n_line)
    my_col = lax.axis_index("col")
    block = lax.div(my_col, n_line) * n_line
    crossed = block + lax.rem(my_col - block + n_line // 2, n_line)

    def ahead(k):
        there = {"row": row_of(flat, lax.rem(deep + k, n_line), n_line)}
        if 2 * k == n_line:
            there["col"] = crossed
        return there

    def aside(k):
        return {"row": row_of(lax.rem(flat + k, n_plane), deep, n_line)}

    own = [
        pltpu.make_async_copy(cells_ref, cells, own_sem.at[0]),
        pltpu.make_async_copy(scale_ref, scale, own_sem.at[1]),
    ]
    for copy in own:
        copy.start()
    barrier = pltpu.get_barrier_semaphore()
    for k in range(1, n_line):
        pl.semaphore_signal(barrier, inc=1, device_id=ahead(k), device_id_type=MESH)
    for k in range(1, n_plane):
        pl.semaphore_signal(barrier, inc=1, device_id=aside(k), device_id_type=MESH)
    for copy in own:
        copy.wait()
    for axis in range(3):
        tiles[0, axis:axis + 1] = cells[axis].astype(jnp.float32)
    tiles[0, 3:4] = scale[...]
    keep = pltpu.make_async_copy(tiles.at[0], out_ref.at[n_plane, 0], own_sem.at[2])
    spare = pltpu.make_async_copy(tiles.at[0], out_ref.at[n_plane, 1], own_sem.at[4])
    keep.start()
    spare.start()
    pl.semaphore_wait(barrier, n_line + n_plane - 2)

    line = []
    for k in ORDER:
        copy = pltpu.make_async_remote_copy(
            src_ref=tiles.at[0], dst_ref=tiles.at[k],
            send_sem=line_send.at[k], recv_sem=line_recv.at[k],
            device_id=ahead(k), device_id_type=MESH,
        )
        copy.start()
        line.append(copy)
    for copy in line:
        copy.wait_recv()
    pivot = p_ref[0]
    col_deep = lax.rem(lax.div(my_col, 2), n_line)
    chosen = jnp.zeros(tiles.shape[1:], jnp.float32)
    column = chosen
    for k in range(n_line):
        deep_at = lax.rem(deep + n_line - k, n_line)
        held = tiles[k]
        chosen = jnp.where(row_of(flat, deep_at, n_line) == pivot, held, chosen)
        column = jnp.where(deep_at == col_deep, held, column)
    picks[0] = chosen
    picks[1] = column
    plane = []
    for k in (7, 6, 5, 4, 3, 2, 1):
        copy = pltpu.make_async_remote_copy(
            src_ref=picks, dst_ref=out_ref.at[k],
            send_sem=plane_send.at[k], recv_sem=plane_recv.at[k],
            device_id=aside(k), device_id_type=MESH,
        )
        copy.start()
        plane.append(copy)
    last = pltpu.make_async_copy(picks, out_ref.at[0], own_sem.at[3])
    last.start()
    keep.wait()
    spare.wait()
    last.wait()
    for copy in line:
        copy.wait_send()
    for copy in plane:
        copy.wait()


def gather_sites(cells, scale, panel):
    width = cells.shape[2]
    n_plane = lax.axis_size("row") // DEPTH
    return pl.pallas_call(
        gather_body,
        out_shape=jax.ShapeDtypeStruct((n_plane + 1, 2, 4, width), jnp.float32),
        in_specs=[pl.BlockSpec(memory_space=pltpu.SMEM)] + [pl.BlockSpec(memory_space=pltpu.HBM)] * 2,
        out_specs=pl.BlockSpec(memory_space=pltpu.HBM),
        scratch_shapes=[
            pltpu.VMEM((3, 1, width), jnp.int32),
            pltpu.VMEM((1, width), jnp.float32),
            pltpu.VMEM((DEPTH, 4, width), jnp.float32),
            pltpu.VMEM((2, 4, width), jnp.float32),
            pltpu.SemaphoreType.DMA((DEPTH,)),
            pltpu.SemaphoreType.DMA((DEPTH,)),
            pltpu.SemaphoreType.DMA((n_plane,)),
            pltpu.SemaphoreType.DMA((n_plane,)),
            pltpu.SemaphoreType.DMA((5,)),
        ],
        compiler_params=pltpu.CompilerParams(collective_id=0, has_side_effects=True),
        name="gather_sites",
    )(panel, cells, scale)


def pick(sites_ref, parts):
    n_plane = sites_ref.shape[0] - 1
    deep, flat = place(DEPTH)
    my_col, n_col = lax.axis_index("col"), lax.axis_size("col")
    pivot = sites_ref[0, 0]
    for k in range(1, n_plane):
        pivot = pivot + sites_ref[k, 0]
    cols = []
    for m in range(parts):
        tile = my_col + m * n_col
        home = lax.div(tile, 2 * DEPTH) * 2 + lax.rem(tile, 2)
        held = sites_ref[0, 1]
        for k in range(1, n_plane):
            held = jnp.where(lax.rem(flat + n_plane - k, n_plane) == home, sites_ref[k, 1], held)
        cols.append(held)
    return pivot, sites_ref[n_plane, 0], cols


def body(p_ref, sites_ref, panel_ref, trail_ref, t_ref, k_ref, f_ref, u_high, u_low, x_high, x_low):
    share, width = panel_ref.shape
    parts = trail_ref.shape[1]
    my_row = lax.axis_index("row")
    my_col = lax.axis_index("col")
    n_col = lax.axis_size("col")
    pivot = p_ref[0]
    piv, mine, cols = pick(sites_ref, parts)
    col_ids = [my_col + m * n_col for m in range(parts)]
    piv_left, piv_right = features(piv)
    my_left, my_right = features(mine)
    rights = [my_right] + [features(one)[1] for one in cols]
    sub = lax.broadcasted_iota(jnp.int32, (width, width), 0)
    lane = lax.broadcasted_iota(jnp.int32, (width, width), 1)
    t_ref[...] = matern(squared(piv_left, piv_right)) + jnp.where(sub == lane, NUGGET, 0.0)
    for m, right in enumerate(rights):
        k_ref[:, m * width:(m + 1) * width] = squared(piv_left, right)
        if m:
            f_ref[:, (m - 1) * width:m * width] = squared(my_left, right)
    scale_r = mine.T[:, 3:4]
    scales = [mine[3:4]] + [one[3:4] for one in cols]

    slopes = [one * INV_LENGTH for one in scales]

    def nugget(same):
        return jnp.where(same, NUGGET, 0.0)

    k_nuggets = [nugget(my_row == pivot)] + [nugget(tid == pivot) for tid in col_ids]
    f_nuggets = [nugget(tid == my_row) for tid in col_ids]
    r8 = lax.broadcasted_iota(jnp.int32, (ROWS, PART), 0)
    l8 = lax.broadcasted_iota(jnp.int32, (ROWS, PART), 1)

    def kernel_rows(ref, g, m, extra, scale, slope, column):
        lo = g * ROWS
        at = lo // PART * PART
        squares = ref[lo:lo + ROWS, m * width:(m + 1) * width]
        length = squares * lax.rsqrt(jnp.maximum(squares, 0.5))
        value = (scale + slope * length) * jnp.exp2(length * (-LOG2E * INV_LENGTH))
        if column is not None:
            value = value * column[lo:lo + ROWS]
        ref[lo:lo + ROWS, m * width:(m + 1) * width] = value
        near = scale[:, at:at + PART] * extra
        if column is not None:
            near = near * column[lo:lo + ROWS]
        spot = ref.at[lo:lo + ROWS, m * width + at:m * width + at + PART]
        spot[...] = value[:, at:at + PART] + jnp.where(l8 == r8 + (lo - at), near, 0.0)

    for g in range(width // ROWS):
        for m in range(parts + 1):
            kernel_rows(k_ref, g, m, k_nuggets[m], scales[m], slopes[m], None)
        for m in range(parts):
            kernel_rows(f_ref, g, m, f_nuggets[m], scales[m + 1], slopes[m + 1], scale_r)
    half = width // 2

    def update(lo, final):
        rows = [ref[lo:lo + half, :width] for ref in (x_high, x_low)]
        for m in range(parts):
            rest = f_ref[:, m * width:(m + 1) * width] - dot3_tn(
                rows, [ref[lo:lo + half, (m + 1) * width:(m + 2) * width] for ref in (x_high, x_low)]
            )
            if final:
                trail_ref[:, m, :] = rest.astype(jnp.bfloat16)
            else:
                f_ref[:, m * width:(m + 1) * width] = rest

    def done(hi):
        if hi % half == 0:
            update(hi - half, hi == width)

    eliminate(t_ref, k_ref, (u_high, u_low), (x_high, x_low), done)
    mine_rows = pl.ds(pl.multiple_of(my_col * share, share), share)
    panel_ref[...] = x_high[mine_rows, :width].astype(jnp.float32) + x_low[mine_rows, :width].astype(jnp.float32)


def eliminate_panel(sites, panel, width, share, parts):
    return pl.pallas_call(
        body,
        out_shape=(
            jax.ShapeDtypeStruct((share, width), jnp.float32),
            jax.ShapeDtypeStruct((width, parts, width), jnp.bfloat16),
        ),
        in_specs=[pl.BlockSpec(memory_space=pltpu.SMEM), pl.BlockSpec(memory_space=pltpu.VMEM)],
        out_specs=[pl.BlockSpec(memory_space=pltpu.VMEM)] * 2,
        scratch_shapes=[
            pltpu.VMEM((width, width), jnp.float32),
            pltpu.VMEM((width, (parts + 1) * width), jnp.float32),
            pltpu.VMEM((width, parts * width), jnp.float32),
            pltpu.VMEM((width, width), jnp.bfloat16),
            pltpu.VMEM((width, width), jnp.bfloat16),
            pltpu.VMEM((width, (parts + 1) * width), jnp.bfloat16),
            pltpu.VMEM((width, (parts + 1) * width), jnp.bfloat16),
        ],
        compiler_params=pltpu.CompilerParams(vmem_limit_bytes=48 << 20),
        name="eliminate_panel",
    )(panel, sites)


def on_device(site_cells, site_scale, panel):
    width = site_cells.shape[2]
    n_row, n_col = lax.axis_size("row"), lax.axis_size("col")
    sites = gather_sites(site_cells, site_scale, panel)
    panel_out, trailing = eliminate_panel(sites, panel, width, width // n_col, n_row // n_col)
    return panel_out.T[None], trailing[None]


def solution(mesh):
    placed = (P(None, None, "row"), P(None, "row"), P())
    return jax.shard_map(
        on_device,
        mesh=mesh,
        in_specs=placed,
        out_specs=(P(None, "row", "col"), P(None, "row", None, "col")),
        check_vma=False,
    )
```

```python
import math
import jax
import jax.numpy as jnp
from jax import lax
from jax.experimental import pallas as pl
from jax.experimental.pallas import tpu as pltpu
from jax.sharding import PartitionSpec as P

MESH = pl.DeviceIdType.MESH
NUGGET = 0.25
INV_LENGTH = 1.7320508075688772 / 12.0
LOG2E = 1.0 / math.log(2.0)
HI = lax.Precision.HIGHEST
PART = 128
HALF = 64
ROWS = 8
DEPTH = 4
ORDER = (2, 1, 3)


def dot(a, b, precision=HI):
    return jnp.dot(a, b, precision=precision, preferred_element_type=jnp.float32)


def dot_tn(a, b, precision=HI):
    return lax.dot_general(a, b, (((0,), (0,)), ((), ())), precision=precision, preferred_element_type=jnp.float32)


def split(a):
    high = a.astype(jnp.bfloat16)
    return high, (a - high.astype(jnp.float32)).astype(jnp.bfloat16)


def dot3(a, b):
    (ah, al), (bh, bl) = a, b
    if bh.shape[0] <= PART:
        return dot(jnp.concatenate([ah, al, ah], axis=1), jnp.concatenate([bh, bh, bl], axis=0), None)
    return dot(ah, bh, None) + (dot(ah, bl, None) + dot(al, bh, None))


def dot3_tn(a, b):
    (ah, al), (bh, bl) = a, b
    if bh.shape[0] <= PART:
        return dot_tn(jnp.concatenate([ah, al, ah], axis=0), jnp.concatenate([bh, bh, bl], axis=0), None)
    return dot_tn(ah, bh, None) + (dot_tn(ah, bl, None) + dot_tn(al, bh, None))


def features(tile):
    x, y, z = tile[0:1], tile[1:2], 2.0 * tile[2:3]
    norm = x * x + y * y + z * z
    high = jnp.floor(norm * (1.0 / 256.0)) * 256.0
    low = norm - high
    one, zero = jnp.ones_like(x), jnp.zeros_like(x)
    left = jnp.concatenate([x, y, z, high, low, one, one, zero], axis=0)
    right = jnp.concatenate([-2.0 * x, -2.0 * y, -2.0 * z, one, one, high, low, zero], axis=0)
    return left, right


def squared(left, right):
    return dot_tn(left, right, lax.Precision.DEFAULT)


def matern(squares):
    radius = squares * lax.rsqrt(jnp.maximum(squares, 0.5)) * INV_LENGTH
    return (1.0 + radius) * jnp.exp2(radius * -LOG2E)


def col(x, k):
    return jnp.broadcast_to(x[:, k:k + 1], (ROWS, PART))


def row(x, j):
    return jnp.broadcast_to(x[j:j + 1, :], (ROWS, PART))


def inverse_factor(block):
    groups, half = PART // ROWS, HALF // ROWS
    sub = lax.broadcasted_iota(jnp.int32, (ROWS, PART), 0)
    lane = lax.broadcasted_iota(jnp.int32, (ROWS, PART), 1)
    t = [block(g) for g in range(groups)]
    out = []
    for base in range(0, groups, half):
        top = base + half
        raw = []
        c = [col(t[base], base * ROWS + k) for k in range(ROWS)]
        for p in range(base, top):
            lo = p * ROWS
            inside = jnp.logical_and(lane >= lo, lane < lo + ROWS)
            steps = []
            diag = jnp.ones((ROWS, PART), jnp.float32)
            own = jnp.where(inside, jnp.where(lane - lo == sub, 1.0, 0.0), t[p])
            last = p + 1 == top
            if not last:
                cc = [col(t[p + 1], lo + k) for k in range(ROWS)]
                cn = [col(t[p + 1], lo + ROWS + k) for k in range(ROWS)]
                tg = jnp.where(inside, 0.0, t[p + 1])
            for j in range(ROWS):
                d = row(c[j], j)
                diag = jnp.where(sub == j, d, diag)
                inv = 1.0 / d
                rc = [row(c[k], j) for k in range(j + 1, ROWS)]
                ra = row(own, j)
                steps.append((inv, rc, ra))
                if j < ROWS - 1:
                    m = jnp.where(sub > j, c[j] * inv, 0.0)
                    for k in range(j + 1, ROWS):
                        c[k] = c[k] - m * rc[k - j - 1]
                    own = own - m * ra
                if not last:
                    m = cc[j] * inv
                    for k in range(ROWS):
                        cn[k] = cn[k] - m * row(cc[j], k)
                    for k in range(j + 1, ROWS):
                        cc[k] = cc[k] - m * rc[k - j - 1]
                    tg = tg - m * ra
            raw.append(own * lax.rsqrt(diag))
            if last:
                break
            t[p + 1] = tg
            c = cn
            for g in range(p + 2, top):
                cc = [col(t[g], lo + k) for k in range(ROWS)]
                tg = jnp.where(inside, 0.0, t[g])
                for j in range(ROWS):
                    inv, rc, ra = steps[j]
                    m = cc[j] * inv
                    for k in range(j + 1, ROWS):
                        cc[k] = cc[k] - m * rc[k - j - 1]
                    tg = tg - m * ra
                t[g] = tg
        for i, r in enumerate(raw):
            out.append(jnp.where(lane < (base + i + 1) * ROWS, r, 0.0))
        if top < groups:
            done = top * ROWS
            u = jnp.concatenate(
                [jnp.where(jnp.logical_or(lane < (base + i + 1) * ROWS, lane >= done), r, 0.0) for i, r in enumerate(raw)],
                axis=0,
            )
            u = split(u)
            update = dot3_tn([v[:, done:] for v in u], u)
            for g in range(top, groups):
                keep = jnp.where(jnp.logical_and(lane >= base * ROWS, lane < done), 0.0, t[g])
                t[g] = keep - update[(g - top) * ROWS:(g - top + 1) * ROWS]
    return jnp.concatenate(out, axis=0)


def eliminate(t_ref, k_ref, u_refs, x_refs, done):
    n = t_ref.shape[0]
    for lo in range(0, n, PART):
        hi = lo + PART
        small = split(inverse_factor(lambda g: t_ref[lo + g * ROWS:lo + (g + 1) * ROWS, lo:hi]))
        if hi < n:
            after = hi + PART
            right = split(dot3(small, split(t_ref[lo:hi, hi:after])))
            t_ref[hi:after, hi:after] = t_ref[hi:after, hi:after] - dot3_tn(right, right)
            for ref, value in zip(u_refs, right):
                ref[lo:hi, hi:after] = value
            if after < n:
                far = split(dot3(small, split(t_ref[lo:hi, after:])))
                t_ref[hi:after, after:] = t_ref[hi:after, after:] - dot3_tn(right, far)
                t_ref[after:, after:] = t_ref[after:, after:] - dot3_tn(far, far)
                for ref, value in zip(u_refs, far):
                    ref[lo:hi, after:] = value
        for ref, value in zip(x_refs, split(dot3(small, split(k_ref[lo:hi, :])))):
            ref[lo:hi, :] = value
        if hi < n:
            k_ref[hi:after, :] = k_ref[hi:after, :] - dot3_tn(
                [ref[:hi, hi:after] for ref in u_refs], [ref[:hi, :] for ref in x_refs]
            )
        done(hi)


def place(n_line):
    my_row = lax.axis_index("row")
    core = lax.rem(my_row, 2)
    deep = lax.rem(lax.div(my_row, 2), n_line)
    flat = lax.div(my_row, 2 * n_line) * 2 + core
    return deep, flat


def row_of(flat, deep, n_line):
    return lax.div(flat, 2) * (2 * n_line) + deep * 2 + lax.rem(flat, 2)


def gather_body(p_ref, cells_ref, scale_ref, out_ref, cells, scale, tiles, picks, line_send, line_recv, plane_send, plane_recv, own_sem):
    n_line, n_plane = tiles.shape[0], out_ref.shape[0] - 1
    deep, flat = place(n_line)
    my_col = lax.axis_index("col")
    block = lax.div(my_col, n_line) * n_line
    crossed = block + lax.rem(my_col - block + n_line // 2, n_line)

    def ahead(k):
        there = {"row": row_of(flat, lax.rem(deep + k, n_line), n_line)}
        if 2 * k == n_line:
            there["col"] = crossed
        return there

    def aside(k):
        return {"row": row_of(lax.rem(flat + k, n_plane), deep, n_line)}

    own = [
        pltpu.make_async_copy(cells_ref, cells, own_sem.at[0]),
        pltpu.make_async_copy(scale_ref, scale, own_sem.at[1]),
    ]
    for copy in own:
        copy.start()
    barrier = pltpu.get_barrier_semaphore()
    for k in range(1, n_line):
        pl.semaphore_signal(barrier, inc=1, device_id=ahead(k), device_id_type=MESH)
    for k in range(1, n_plane):
        pl.semaphore_signal(barrier, inc=1, device_id=aside(k), device_id_type=MESH)
    for copy in own:
        copy.wait()
    for axis in range(3):
        tiles[0, axis:axis + 1] = cells[axis].astype(jnp.float32)
    tiles[0, 3:4] = scale[...]
    keep = pltpu.make_async_copy(tiles.at[0], out_ref.at[n_plane, 0], own_sem.at[2])
    spare = pltpu.make_async_copy(tiles.at[0], out_ref.at[n_plane, 1], own_sem.at[4])
    keep.start()
    spare.start()
    pl.semaphore_wait(barrier, n_line + n_plane - 2)

    line = []
    for k in ORDER:
        copy = pltpu.make_async_remote_copy(
            src_ref=tiles.at[0], dst_ref=tiles.at[k],
            send_sem=line_send.at[k], recv_sem=line_recv.at[k],
            device_id=ahead(k), device_id_type=MESH,
        )
        copy.start()
        line.append(copy)
    for copy in line:
        copy.wait_recv()
    pivot = p_ref[0]
    col_deep = lax.rem(lax.div(my_col, 2), n_line)
    chosen = jnp.zeros(tiles.shape[1:], jnp.float32)
    column = chosen
    for k in range(n_line):
        deep_at = lax.rem(deep + n_line - k, n_line)
        held = tiles[k]
        chosen = jnp.where(row_of(flat, deep_at, n_line) == pivot, held, chosen)
        column = jnp.where(deep_at == col_deep, held, column)
    picks[0] = chosen
    picks[1] = column
    plane = []
    for k in (7, 6, 5, 4, 3, 2, 1):
        copy = pltpu.make_async_remote_copy(
            src_ref=picks, dst_ref=out_ref.at[k],
            send_sem=plane_send.at[k], recv_sem=plane_recv.at[k],
            device_id=aside(k), device_id_type=MESH,
        )
        copy.start()
        plane.append(copy)
    last = pltpu.make_async_copy(picks, out_ref.at[0], own_sem.at[3])
    last.start()
    keep.wait()
    spare.wait()
    last.wait()
    for copy in line:
        copy.wait_send()
    for copy in plane:
        copy.wait()


def gather_sites(cells, scale, panel):
    width = cells.shape[2]
    n_plane = lax.axis_size("row") // DEPTH
    return pl.pallas_call(
        gather_body,
        out_shape=jax.ShapeDtypeStruct((n_plane + 1, 2, 4, width), jnp.float32),
        in_specs=[pl.BlockSpec(memory_space=pltpu.SMEM)] + [pl.BlockSpec(memory_space=pltpu.HBM)] * 2,
        out_specs=pl.BlockSpec(memory_space=pltpu.HBM),
        scratch_shapes=[
            pltpu.VMEM((3, 1, width), jnp.int32),
            pltpu.VMEM((1, width), jnp.float32),
            pltpu.VMEM((DEPTH, 4, width), jnp.float32),
            pltpu.VMEM((2, 4, width), jnp.float32),
            pltpu.SemaphoreType.DMA((DEPTH,)),
            pltpu.SemaphoreType.DMA((DEPTH,)),
            pltpu.SemaphoreType.DMA((n_plane,)),
            pltpu.SemaphoreType.DMA((n_plane,)),
            pltpu.SemaphoreType.DMA((5,)),
        ],
        compiler_params=pltpu.CompilerParams(collective_id=0, has_side_effects=True),
        name="gather_sites",
    )(panel, cells, scale)


def pick(sites_ref, parts):
    n_plane = sites_ref.shape[0] - 1
    deep, flat = place(DEPTH)
    my_col, n_col = lax.axis_index("col"), lax.axis_size("col")
    pivot = sites_ref[0, 0]
    for k in range(1, n_plane):
        pivot = pivot + sites_ref[k, 0]
    cols = []
    for m in range(parts):
        tile = my_col + m * n_col
        home = lax.div(tile, 2 * DEPTH) * 2 + lax.rem(tile, 2)
        held = sites_ref[0, 1]
        for k in range(1, n_plane):
            held = jnp.where(lax.rem(flat + n_plane - k, n_plane) == home, sites_ref[k, 1], held)
        cols.append(held)
    return pivot, sites_ref[n_plane, 0], cols


def body(p_ref, sites_ref, panel_ref, trail_ref, t_ref, k_ref, f_ref, u_high, u_low, x_high, x_low):
    share, width = panel_ref.shape
    parts = trail_ref.shape[1]
    my_row = lax.axis_index("row")
    my_col = lax.axis_index("col")
    n_col = lax.axis_size("col")
    pivot = p_ref[0]
    piv, mine, cols = pick(sites_ref, parts)
    col_ids = [my_col + m * n_col for m in range(parts)]
    piv_left, piv_right = features(piv)
    my_left, my_right = features(mine)
    rights = [my_right] + [features(one)[1] for one in cols]
    sub = lax.broadcasted_iota(jnp.int32, (width, width), 0)
    lane = lax.broadcasted_iota(jnp.int32, (width, width), 1)
    t_ref[...] = matern(squared(piv_left, piv_right)) + jnp.where(sub == lane, NUGGET, 0.0)
    for m, right in enumerate(rights):
        k_ref[:, m * width:(m + 1) * width] = squared(piv_left, right)
        if m:
            f_ref[:, (m - 1) * width:m * width] = squared(my_left, right)
    scale_r = mine.T[:, 3:4]
    scales = [mine[3:4]] + [one[3:4] for one in cols]

    slopes = [one * INV_LENGTH for one in scales]

    def nugget(same):
        return jnp.where(same, NUGGET, 0.0)

    k_nuggets = [nugget(my_row == pivot)] + [nugget(tid == pivot) for tid in col_ids]
    f_nuggets = [nugget(tid == my_row) for tid in col_ids]
    r8 = lax.broadcasted_iota(jnp.int32, (ROWS, PART), 0)
    l8 = lax.broadcasted_iota(jnp.int32, (ROWS, PART), 1)

    def kernel_rows(ref, g, m, extra, scale, slope, column):
        lo = g * ROWS
        at = lo // PART * PART
        squares = ref[lo:lo + ROWS, m * width:(m + 1) * width]
        length = squares * lax.rsqrt(jnp.maximum(squares, 0.5))
        value = (scale + slope * length) * jnp.exp2(length * (-LOG2E * INV_LENGTH))
        if column is not None:
            value = value * column[lo:lo + ROWS]
        ref[lo:lo + ROWS, m * width:(m + 1) * width] = value
        near = scale[:, at:at + PART] * extra
        if column is not None:
            near = near * column[lo:lo + ROWS]
        spot = ref.at[lo:lo + ROWS, m * width + at:m * width + at + PART]
        spot[...] = value[:, at:at + PART] + jnp.where(l8 == r8 + (lo - at), near, 0.0)

    for g in range(width // ROWS):
        for m in range(parts + 1):
            kernel_rows(k_ref, g, m, k_nuggets[m], scales[m], slopes[m], None)
        for m in range(parts):
            kernel_rows(f_ref, g, m, f_nuggets[m], scales[m + 1], slopes[m + 1], scale_r)
    half = width // 2

    def update(lo, final):
        rows = [ref[lo:lo + half, :width] for ref in (x_high, x_low)]
        for m in range(parts):
            rest = f_ref[:, m * width:(m + 1) * width] - dot3_tn(
                rows, [ref[lo:lo + half, (m + 1) * width:(m + 2) * width] for ref in (x_high, x_low)]
            )
            if final:
                trail_ref[:, m, :] = rest.astype(jnp.bfloat16)
            else:
                f_ref[:, m * width:(m + 1) * width] = rest

    def done(hi):
        if hi % half == 0:
            update(hi - half, hi == width)

    eliminate(t_ref, k_ref, (u_high, u_low), (x_high, x_low), done)
    mine_rows = pl.ds(pl.multiple_of(my_col * share, share), share)
    panel_ref[...] = x_high[mine_rows, :width].astype(jnp.float32) + x_low[mine_rows, :width].astype(jnp.float32)


def eliminate_panel(sites, panel, width, share, parts):
    return pl.pallas_call(
        body,
        out_shape=(
            jax.ShapeDtypeStruct((share, width), jnp.float32),
            jax.ShapeDtypeStruct((width, parts, width), jnp.bfloat16),
        ),
        in_specs=[pl.BlockSpec(memory_space=pltpu.SMEM), pl.BlockSpec(memory_space=pltpu.VMEM)],
        out_specs=[pl.BlockSpec(memory_space=pltpu.VMEM)] * 2,
        scratch_shapes=[
            pltpu.VMEM((width, width), jnp.float32),
            pltpu.VMEM((width, (parts + 1) * width), jnp.float32),
            pltpu.VMEM((width, parts * width), jnp.float32),
            pltpu.VMEM((width, width), jnp.bfloat16),
            pltpu.VMEM((width, width), jnp.bfloat16),
            pltpu.VMEM((width, (parts + 1) * width), jnp.bfloat16),
            pltpu.VMEM((width, (parts + 1) * width), jnp.bfloat16),
        ],
        compiler_params=pltpu.CompilerParams(vmem_limit_bytes=48 << 20),
        name="eliminate_panel",
    )(panel, sites)


def on_device(site_cells, site_scale, panel):
    width = site_cells.shape[2]
    n_row, n_col = lax.axis_size("row"), lax.axis_size("col")
    sites = gather_sites(site_cells, site_scale, panel)
    panel_out, trailing = eliminate_panel(sites, panel, width, width // n_col, n_row // n_col)
    return panel_out.T[None], trailing[None]


def solution(mesh):
    placed = (P(None, None, "row"), P(None, "row"), P())
    return jax.shard_map(
        on_device,
        mesh=mesh,
        in_specs=placed,
        out_specs=(P(None, "row", "col"), P(None, "row", None, "col")),
        check_vma=False,
    )
```
